512 devices in a mesh: lon: 64 (over x_hi, z, core), tp: 8 (over y, x_lo).
Axes of the slice: x: 4 (x_hi: 2, x_lo: 2; x = x_hi * 2 + x_lo), y: 4, z: 16, core: 2. Of those that a mesh axis runs over, the one named last changes fastest.
Arguments:
- image_tokens: bfloat16 [16384, 3072], P('lon', 'tp'), may hold values from -6 to 6
- style_tokens: bfloat16 [2048, 3072], P('lon', 'tp'), may hold values from -6 to 6
- qkv_weight: bfloat16 [3, 3072, 2048], P(None, 'lon', 'tp'), may hold values from -0.109375 to 0.109375
- out_weight: bfloat16 [2048, 3072], P('tp', 'lon'), may hold values from -0.125 to 0.125
- query_gain: float32 [128], replicated, may hold values from 0.6 to 9, as said below
- key_gain: float32 [128], replicated, may hold values from 0.6 to 9, as said below
- attend_flags: int32 [64, 1], P('lon'), may hold values from 0 to 1
Outputs:
- mixed: bfloat16 [16384, 3072], P('lon', 'tp')
The draws below stay inside these ranges and needn't reach their ends.
Inputs may be any that keep to these rules, and one draw needn't show every extreme that they name: `query_gain`: positive gains. `key_gain`: positive gains.
All inputs are finite; a program needn't handle non-finite values.
Results may differ from the reference program's by a relative error of at most 0.015.
The reference program's roundings to bfloat16 on the way (of `weights` and `attended`) count: a program that leaves them out, or rounds other values in their place, can miss the bound.
Values may be sent and summed in bfloat16 or wider, within the bound.
No kernel may reach another device: no remote copies, remote signals or barrier semaphores. Data moves between devices by JAX's collectives and lax.ppermute only.
A program may use at most 64 MiB of HBM per device.

```python
import math
import jax
import jax.numpy as jnp
from jax import lax

D = 3072
HEADS = 16
HEAD = 128
TOK_DEV = 256
HD = 2048
SLABS = 64
TOKENS = 16384
REF = 2048


def draw_query_gain(key, part):
    inner = jax.random.fold_in(key, 11)
    return jax.random.uniform(inner, (HEAD,), jnp.float32, 0.6, 1.6)


def draw_key_gain(key, part):
    inner = jax.random.fold_in(key, 23)
    return jax.random.uniform(inner, (HEAD,), jnp.float32, 0.6, 1.6)


def set_ends(entries, stream_key, low, top_value):
    dims = entries.shape
    index_at = [jax.random.randint(jax.random.fold_in(stream_key, axis), (), 0, dims[axis]) for axis in range(len(dims))]
    entries = entries.at[tuple(index_at)].set(low)
    longest = dims.index(max(dims))
    index_at[longest] = (index_at[longest] + 1) % dims[longest]
    return entries.at[tuple(index_at)].set(top_value)


def level_of(key, extent, pieces, least, largest):
    factor_of = 1.0
    for axis_at, parts in pieces:
        heights = jax.random.uniform(jax.random.fold_in(jax.random.fold_in(key, 6), axis_at), (parts,), jnp.float32, least / len(pieces), largest / len(pieces))
        factor_of = factor_of * jnp.repeat(jnp.exp(heights), extent[axis_at] // parts).reshape((-1,) + (1,) * (len(extent) - 1 - axis_at))
    return factor_of


def gaussian(rng, extent, deviation, most, cuts=(), kind=jnp.bfloat16):
    drawn = deviation * jax.random.normal(rng, extent, jnp.float32)
    if cuts:
        drawn = drawn * level_of(rng, extent, cuts, -0.22, 0.18)
    return jnp.clip(drawn, -most, most).astype(kind)


def setup_inputs(seed: int = 0) -> dict:
    splits = jax.random.split(jax.random.key(seed), 8)
    return {
        "image_tokens": gaussian(splits[0], (TOKENS, D), 1.0, 6.0, ((0, 64), (1, 8))),
        "style_tokens": gaussian(splits[1], (REF, D), 1.0, 6.0, ((0, 64), (1, 8))),
        "qkv_weight": gaussian(splits[2], (3, D, HD), D ** -0.5, 0.109375, ((1, 64), (2, 8))),
        "out_weight": gaussian(splits[3], (HD, D), HD ** -0.5, 0.125, ((0, 8), (1, 64))),
        "query_gain": draw_query_gain(jax.random.fold_in(splits[7], 71), 0),
        "key_gain": draw_key_gain(jax.random.fold_in(splits[7], 71), 0),
        "attend_flags": set_ends(jax.random.randint(splits[6], (SLABS, 1), 0, 2), jax.random.fold_in(splits[6], 1), 0, 1).astype(jnp.int32),
    }


def head_norm(values, gain):
    return values * lax.rsqrt(lax.optimization_barrier(jnp.mean(values * values, axis=-1, keepdims=True)) + 1e-06) * gain

def reference(image_tokens, style_tokens, qkv_weight, out_weight, query_gain, key_gain, attend_flags):
    count = image_tokens.shape[0]
    slab_count = count // TOK_DEV
    ref_count = style_tokens.shape[0]
    proj = [jnp.dot(image_tokens, qkv_weight[j], preferred_element_type=jnp.float32) for j in range(3)]
    query = head_norm(proj[0].reshape(count, HEADS, HEAD), query_gain).astype(jnp.bfloat16)
    keys = head_norm(proj[1].reshape(count, HEADS, HEAD), key_gain).astype(jnp.bfloat16)
    values = proj[2].reshape(count, HEADS, HEAD).astype(jnp.bfloat16)
    ref_key = jnp.dot(style_tokens, qkv_weight[1], preferred_element_type=jnp.float32)
    ref_key = head_norm(ref_key.reshape(ref_count, HEADS, HEAD), key_gain).astype(jnp.bfloat16)
    ref_value = jnp.dot(style_tokens, qkv_weight[2], preferred_element_type=jnp.float32)
    ref_value = ref_value.reshape(ref_count, HEADS, HEAD).astype(jnp.bfloat16)
    query_slabs = query.reshape(slab_count, TOK_DEV, HEADS, HEAD)
    key_slabs = keys.reshape(slab_count, TOK_DEV, HEADS, HEAD)
    value_slabs = values.reshape(slab_count, TOK_DEV, HEADS, HEAD)

    def one_slab(packed):
        query_block, key_prev, key_own, key_next, value_prev, value_own, value_next, flags = packed
        key_set = jnp.concatenate([key_prev, key_own, key_next, ref_key], axis=0).astype(jnp.float32)
        value_set = jnp.concatenate([value_prev, value_own, value_next, ref_value], axis=0).astype(jnp.float32)
        scores = jnp.einsum('qhe,khe->hqk', query_block.astype(jnp.float32), key_set) / math.sqrt(HEAD)
        allowed = jnp.concatenate([jnp.ones((3 * TOK_DEV,), bool), jnp.full((ref_count,), flags[0] > 0)])
        scores = jnp.where(allowed[None, None, :], scores, -1e+30)
        peak = lax.optimization_barrier(jnp.max(scores, axis=-1, keepdims=True))
        expo = jnp.exp(scores - peak)
        weights = (expo / lax.optimization_barrier(jnp.sum(expo, axis=-1, keepdims=True))).astype(jnp.bfloat16)
        result = jnp.einsum('hqk,khe->qhe', weights.astype(jnp.float32), value_set)
        return result.astype(jnp.bfloat16).reshape(TOK_DEV, HEADS * HEAD)
    attended = lax.map(one_slab, (query_slabs, jnp.roll(key_slabs, 1, axis=0), key_slabs, jnp.roll(key_slabs, -1, axis=0), jnp.roll(value_slabs, 1, axis=0), value_slabs, jnp.roll(value_slabs, -1, axis=0), attend_flags))
    attended = attended.reshape(count, HEADS * HEAD)
    return jnp.dot(attended, out_weight, preferred_element_type=jnp.float32).astype(jnp.bfloat16)
```

```python
import math

import jax
import jax.numpy as jnp
from jax import lax
from jax.experimental import pallas as pl
from jax.experimental.pallas import tpu as pltpu
from jax.sharding import Mesh, PartitionSpec as P

HEAD = 128
AXES = ("x_hi", "z", "core", "y", "x_lo")
LON = ("x_hi", "z", "core")
TP = ("y", "x_lo")
F32 = jnp.float32
BF16 = jnp.bfloat16


def spread(block, axes):
    count = lax.axis_size(axes)
    return lax.all_to_all(
        jnp.broadcast_to(block[None], (count,) + block.shape), axes, 0, 0, tiled=True
    )


def unit(values, gain):
    return values * lax.rsqrt(jnp.mean(values * values, axis=-1, keepdims=True) + 1e-06) * gain


def pack_kernel(w_ref, o_ref, out_ref):
    copies = out_ref.shape[0] * HEAD // w_ref.shape[2]
    for c in range(w_ref.shape[2] // HEAD):
        lanes = pl.ds(c * HEAD, HEAD)
        row = jnp.concatenate(
            [w_ref[1, :, lanes], w_ref[2, :, lanes], w_ref[0, :, lanes], o_ref[:, lanes]], axis=1
        )
        for r in range(copies):
            out_ref[r * (w_ref.shape[2] // HEAD) + c] = row


def pack(w, o, copies):
    heads = w.shape[2] // HEAD
    return pl.pallas_call(
        pack_kernel,
        out_shape=jax.ShapeDtypeStruct((copies * heads, w.shape[1], 4 * HEAD), BF16),
        name="pack",
    )(w, o)


def project_kernel(
    x_ref, y_ref, s_ref, w_ref, qg_ref, kg_ref, kvx_ref, kvy_ref, qx_ref, qy_ref, skv_ref, acc, sacc
):
    step = pl.program_id(0)
    pieces, count, width = x_ref.shape
    groups, _, rows, _ = s_ref.shape

    @pl.when(step == 0)
    def _():
        acc[...] = jnp.zeros_like(acc)
        sacc[...] = jnp.zeros_like(sacc)

    w = w_ref[...]
    s = jnp.concatenate([s_ref[:, i].reshape(groups * rows, width) for i in range(pieces)], axis=1)
    sacc[...] += jnp.dot(s, w[:, : 2 * HEAD], preferred_element_type=F32)
    for i, t_ref in enumerate((x_ref, y_ref)):
        t = jnp.concatenate([t_ref[j] for j in range(pieces)], axis=1)
        acc[i] += jnp.dot(t, w, preferred_element_type=F32)

    @pl.when(step == pl.num_programs(0) - 1)
    def _():
        kg, qg = kg_ref[...], qg_ref[...]
        skv_ref[:, :HEAD] = unit(sacc[:, :HEAD], kg).astype(BF16)
        skv_ref[:, HEAD:] = sacc[:, HEAD:].astype(BF16)
        for i, (kv_ref, q_ref) in enumerate(((kvx_ref, qx_ref), (kvy_ref, qy_ref))):
            kv_ref[:, :HEAD] = unit(acc[i, :, :HEAD], kg).astype(BF16)
            kv_ref[:, HEAD:] = acc[i, :, HEAD : 2 * HEAD].astype(BF16)
            q_ref[...] = unit(acc[i, :, 2 * HEAD :], qg).astype(BF16)


def project(x, y, s, w, query_gain, key_gain):
    parts, count, width = x.shape
    groups, _, rows, _ = s.shape
    pieces = 2
    slab = pl.BlockSpec((pieces, count, width), lambda i: (i, 0, 0))
    gain = pl.BlockSpec((1, HEAD), lambda i: (0, 0))

    def out(tokens, wide):
        spec = pl.BlockSpec((tokens, wide * HEAD), lambda i: (0, 0))
        return spec, jax.ShapeDtypeStruct((tokens, wide * HEAD), BF16)

    outs = [out(count, 2), out(count, 2), out(count, 1), out(count, 1), out(groups * rows, 2)]
    return pl.pallas_call(
        project_kernel,
        grid=(parts // pieces,),
        in_specs=[
            slab,
            slab,
            pl.BlockSpec((groups, pieces, rows, width), lambda i: (0, i, 0, 0)),
            pl.BlockSpec((pieces * width, 3 * HEAD), lambda i: (i, 0)),
            gain,
            gain,
        ],
        out_specs=[o[0] for o in outs],
        out_shape=[o[1] for o in outs],
        scratch_shapes=[
            pltpu.VMEM((2, count, 3 * HEAD), F32),
            pltpu.VMEM((groups * rows, 2 * HEAD), F32),
        ],
        compiler_params=pltpu.CompilerParams(vmem_limit_bytes=16 << 20),
        name="project",
    )(x, y, s, w, query_gain, key_gain)


NT = (((1,), (1,)), ((), ()))


def attend_kernel(
    fx_ref, fy_ref, qx_ref, qy_ref, kvx_ref, kvy_ref, hx_ref, hy_ref, s_ref, ox_ref, oy_ref, near, q
):
    i = pl.program_id(0)
    count = kvx_ref.shape[0]

    @pl.when(i == 0)
    def _():
        near[pl.ds(0, count)] = kvx_ref[...]
        near[pl.ds(count, count)] = kvy_ref[...]
        near[pl.ds(2 * count, count)] = hx_ref[...]
        q[...] = qx_ref[...]

    @pl.when(i == 1)
    def _():
        near[pl.ds(2 * count, count)] = hy_ref[...]
        q[...] = qy_ref[...]

    flag = jnp.where(i == 0, fx_ref[0, 0], fy_ref[0, 0])
    scale = 1.0 / math.sqrt(HEAD)
    close = lax.dot_general(q[...], near[:, :HEAD], NT, preferred_element_type=F32) * scale
    far = lax.dot_general(q[...], s_ref[:, :HEAD], NT, preferred_element_type=F32) * scale
    far = jnp.where(flag > 0, far, -1e30)
    peak = jnp.maximum(
        jnp.max(close, axis=-1, keepdims=True), jnp.max(far, axis=-1, keepdims=True)
    )
    close = jnp.exp(close - peak)
    far = jnp.exp(far - peak)
    total = jnp.sum(close, axis=-1, keepdims=True) + jnp.sum(far, axis=-1, keepdims=True)
    share = 1.0 / total
    out = jnp.dot((close * share).astype(BF16), near[:, HEAD:], preferred_element_type=F32)
    out += jnp.dot((far * share).astype(BF16), s_ref[:, HEAD:], preferred_element_type=F32)
    out = out.astype(BF16)

    @pl.when(i == 0)
    def _():
        ox_ref[...] = out

    @pl.when(i == 1)
    def _():
        oy_ref[...] = out


def attend(flags, queries, kvs, halos, style):
    count = queries[0].shape[0]

    def whole(array):
        return pl.BlockSpec(array.shape, lambda i: (0, 0))

    operands = [*queries, *kvs, *halos, style]
    return pl.pallas_call(
        attend_kernel,
        grid=(2,),
        in_specs=[pl.BlockSpec(memory_space=pltpu.SMEM)] * 2 + [whole(a) for a in operands],
        out_specs=[whole(q) for q in queries],
        out_shape=[jax.ShapeDtypeStruct(q.shape, BF16) for q in queries],
        scratch_shapes=[
            pltpu.VMEM((3 * count, 2 * HEAD), BF16),
            pltpu.VMEM((count, HEAD), BF16),
        ],
        compiler_params=pltpu.CompilerParams(vmem_limit_bytes=24 << 20),
        name="attend",
    )(*flags, *operands)


def mix_kernel(ax_ref, ay_ref, wx_ref, wy_ref, o_ref):
    a = jnp.concatenate([ax_ref[...], ay_ref[...]], axis=1)
    w = jnp.concatenate([wx_ref[...], wy_ref[...]], axis=1)
    o_ref[0] = lax.dot_general(a, w, NT, preferred_element_type=F32).astype(BF16)


def mix(attended, panels, columns, parts):
    count = attended[0].shape[0]
    width = panels[0].shape[0] // parts
    rows = pl.BlockSpec((count, HEAD), lambda i: (0, 0))
    return pl.pallas_call(
        mix_kernel,
        grid=(parts,),
        in_specs=[rows, rows]
        + [pl.BlockSpec((width, HEAD), lambda i, c=c: (i, c)) for c in columns],
        out_specs=pl.BlockSpec((1, count, width), lambda i: (i, 0, 0)),
        out_shape=jax.ShapeDtypeStruct((parts, count, width), BF16),
        compiler_params=pltpu.CompilerParams(vmem_limit_bytes=12 << 20),
        name="mix",
    )(*attended, *panels)


def local(image_tokens, style_tokens, qkv_weight, out_weight, query_gain, key_gain, attend_flags):
    parts = lax.axis_size(TP)
    cores = lax.axis_size("core")
    halves = lax.axis_size("x_hi")
    rows = lax.axis_size("z")
    depth = qkv_weight.shape[1]

    def swap(block):
        return lax.ppermute(block, "core", [(0, 1), (1, 0)])

    mine = pack(qkv_weight, out_weight.T, halves)
    plane = lax.all_to_all(mine, ("x_hi", "core"), 0, 0, tiled=True)
    plane = plane.reshape(halves, cores * depth, 4 * HEAD)
    with jax.named_scope("panel"):
        panel = lax.all_gather(plane, "z", axis=1, tiled=True).reshape(-1, 4 * HEAD)

    image_tokens, style_tokens, attend_flags, _ = lax.optimization_barrier(
        (image_tokens, style_tokens, attend_flags, plane)
    )
    with jax.named_scope("image"):
        own = spread(image_tokens, TP)
    other = swap(own)
    with jax.named_scope("style"):
        style = spread(style_tokens, ("x_hi", "core") + TP)
    style = style.reshape((halves * cores, parts) + style_tokens.shape)
    flags = (attend_flags, swap(attend_flags))

    kvx, kvy, qx, qy, style_kv = project(
        own, other, style, panel, query_gain.reshape(1, HEAD), key_gain.reshape(1, HEAD)
    )
    with jax.named_scope("far"):
        far = spread(style_kv, "z").reshape(-1, 2 * HEAD)
    chips = halves * rows
    outward = [
        (c * cores + k, (c + 1 - 2 * k) % chips * cores + k) for c in range(chips) for k in (0, 1)
    ]
    inward = [
        (c * cores + k, (c - 1 + 2 * k) % chips * cores + k) for c in range(chips) for k in (0, 1)
    ]
    halo_x = lax.ppermute(kvy, LON, outward)
    halo_y = lax.ppermute(kvx, LON, inward)
    out_panel = swap(panel[:, 3 * HEAD :])

    ax, ay = attend(flags, (qx, qy), (kvx, kvy), (halo_x, halo_y), far)
    shares = mix((ax, swap(ay)), (panel, out_panel), (3, 0), parts)
    shares = lax.all_to_all(shares, TP, 0, 0, tiled=True)
    return jnp.sum(shares.astype(F32), axis=0).astype(BF16)


def solution(mesh):
    fine = Mesh(mesh.devices.reshape(2, 16, 2, 4, 2), AXES)
    in_specs = (
        P(LON, TP),
        P(LON, TP),
        P(None, LON, TP),
        P(TP, LON),
        P(),
        P(),
        P(LON, None),
    )
    return jax.shard_map(
        local, mesh=fine, in_specs=in_specs, out_specs=P(LON, TP), check_vma=False
    )
```

```python
import functools
import math

import jax
import jax.numpy as jnp
from jax import lax
from jax.experimental import pallas as pl
from jax.experimental.pallas import tpu as pltpu
from jax.sharding import Mesh, PartitionSpec as P


HEAD = 128
AXES = ("x_hi", "z_hi", "z_lo", "core", "y", "x_lo")
Z = ("z_hi", "z_lo")
LON = ("x_hi",) + Z + ("core",)
TP = ("y", "x_lo")
F32 = jnp.float32
BF16 = jnp.bfloat16


def spread(block, axes):
    count = lax.axis_size(axes)
    return lax.all_to_all(
        jnp.broadcast_to(block[None], (count,) + block.shape), axes, 0, 0, tiled=True
    )


def unit(values, gain):
    return values * lax.rsqrt(jnp.mean(values * values, axis=-1, keepdims=True) + 1e-06) * gain


def pack_kernel(w_ref, o_ref, out_ref):
    copies = out_ref.shape[0] * HEAD // w_ref.shape[2]
    for c in range(w_ref.shape[2] // HEAD):
        lanes = pl.ds(c * HEAD, HEAD)
        row = jnp.concatenate(
            [w_ref[1, :, lanes], w_ref[2, :, lanes], w_ref[0, :, lanes], o_ref[:, lanes]], axis=1
        )
        for r in range(copies):
            out_ref[r * (w_ref.shape[2] // HEAD) + c] = row


def pack(w, o, copies):
    heads = w.shape[2] // HEAD
    return pl.pallas_call(
        pack_kernel,
        out_shape=jax.ShapeDtypeStruct((copies * heads, w.shape[1], 4 * HEAD), BF16),
        name="pack",
    )(w, o)


def project_kernel(
    me_ref,
    x_ref,
    y_ref,
    sx_ref,
    sy_ref,
    w_ref,
    qg_ref,
    kg_ref,
    forward_ref,
    backward_ref,
    low_ref,
    high_ref,
    q_ref,
    acc,
    sacc,
    weights,
    arrived,
):
    step = pl.program_id(0)
    pieces, count, width = x_ref.shape
    groups, _, rows, _ = sx_ref.shape

    def fetch(i):
        lines = pl.ds(i * pieces * width, pieces * width)
        return pltpu.make_async_copy(
            w_ref.at[lines, pl.ds(0, 3 * HEAD)], weights.at[i], arrived.at[i]
        )

    @pl.when(step == 0)
    def _():
        for i in range(weights.shape[0]):
            fetch(i).start()
        acc[...] = jnp.zeros_like(acc)
        sacc[...] = jnp.zeros_like(sacc)

    fetch(step).wait()
    w = weights[step]
    for i, s_ref in enumerate((sx_ref, sy_ref)):
        for g in range(groups):
            s = jnp.concatenate([s_ref[g, j] for j in range(pieces)], axis=1)
            sacc[pl.ds((i * groups + g) * rows, rows)] += jnp.dot(
                s, w[:, : 2 * HEAD], preferred_element_type=F32
            )
    for i, t_ref in enumerate((x_ref, y_ref)):
        t = jnp.concatenate([t_ref[j] for j in range(pieces)], axis=1)
        acc[i] += jnp.dot(t, w, preferred_element_type=F32)

    @pl.when(step == pl.num_programs(0) - 1)
    def _():
        kg, qg = kg_ref[...], qg_ref[...]
        far = 2 * groups * rows
        for half, part_ref in enumerate((low_ref, high_ref)):
            lines = pl.ds(half * far // 2, far // 2)
            k = unit(sacc[lines, :HEAD], kg).astype(BF16)
            v = sacc[lines, HEAD:].astype(BF16)
            for out_ref in (forward_ref, backward_ref):
                out_ref[lines, :HEAD] = k
                out_ref[lines, HEAD:] = v
            part_ref[:, :HEAD] = k
            part_ref[:, HEAD:] = v
        me = me_ref[0]
        lines = pl.ds(far, count)
        for slab, out_ref in enumerate((backward_ref, forward_ref)):
            mine = acc[slab ^ me]
            out_ref[lines, :HEAD] = unit(mine[:, :HEAD], kg).astype(BF16)
            out_ref[lines, HEAD:] = mine[:, HEAD : 2 * HEAD].astype(BF16)
            q_ref[slab] = unit(mine[:, 2 * HEAD :], qg).astype(BF16)


def project(me, slabs, styles, w, query_gain, key_gain):
    parts, count, width = slabs[0].shape
    groups, _, rows, _ = styles[0].shape
    pieces = 2
    far = 2 * groups * rows
    slab = pl.BlockSpec((pieces, count, width), lambda i: (i, 0, 0))
    style = pl.BlockSpec((groups, pieces, rows, width), lambda i: (0, i, 0, 0))
    gain = pl.BlockSpec((1, HEAD), lambda i: (0, 0))

    def out(*shape):
        spec = pl.BlockSpec(shape, lambda i: (0,) * len(shape))
        return spec, jax.ShapeDtypeStruct(shape, BF16)

    pair = (far + count, 2 * HEAD)
    part = (far // 2, 2 * HEAD)
    outs = [out(*pair), out(*pair), out(*part), out(*part), out(2, count, HEAD)]
    return pl.pallas_call(
        project_kernel,
        grid=(parts // pieces,),
        in_specs=[
            pl.BlockSpec(memory_space=pltpu.SMEM),
            slab,
            slab,
            style,
            style,
            pl.BlockSpec(memory_space=pltpu.HBM),
            gain,
            gain,
        ],
        out_specs=[o[0] for o in outs],
        out_shape=[o[1] for o in outs],
        scratch_shapes=[
            pltpu.VMEM((2, count, 3 * HEAD), F32),
            pltpu.VMEM((far, 2 * HEAD), F32),
            pltpu.VMEM((parts // pieces, pieces * width, 3 * HEAD), BF16),
            pltpu.SemaphoreType.DMA((parts // pieces,)),
        ],
        compiler_params=pltpu.CompilerParams(vmem_limit_bytes=58 << 20),
        name="project",
    )(me, *slabs, *styles, w, query_gain, key_gain)


NT = (((1,), (1,)), ((), ()))


def attend_kernel(
    me_ref,
    fx_ref,
    fy_ref,
    q_ref,
    forward_ref,
    backward_ref,
    before_ref,
    after_ref,
    low_ref,
    high_ref,
    ox_ref,
    oy_ref,
    near,
):
    i = pl.program_id(0)
    me = me_ref[0]
    count = q_ref.shape[1]
    style = forward_ref.shape[0] - count
    slab = pl.ds(style, count)

    @pl.when(i == 0)
    def _():
        near[pl.ds(0, count)] = backward_ref[slab]
        near[pl.ds(count, count)] = forward_ref[slab]
        near[pl.ds(2 * count, count)] = before_ref[slab]

    @pl.when(i == 1)
    def _():
        near[pl.ds(2 * count, count)] = after_ref[slab]

    flag = jnp.where(i == me, fx_ref[0, 0], fy_ref[0, 0])
    scale = 1.0 / math.sqrt(HEAD)
    q = q_ref[0]
    lines = pl.ds(0, style)
    refs = [near, *(r.at[lines] for r in (forward_ref, before_ref, after_ref)), low_ref, high_ref]
    scores = []
    for n, ref in enumerate(refs):
        part = lax.dot_general(q, ref[:, :HEAD], NT, preferred_element_type=F32) * scale
        scores.append(jnp.where(flag > 0, part, -1e30) if n else part)
    peak = functools.reduce(jnp.maximum, [jnp.max(s, axis=-1, keepdims=True) for s in scores])
    expo = [jnp.exp(s - peak) for s in scores]
    share = 1.0 / sum(jnp.sum(e, axis=-1, keepdims=True) for e in expo)
    out = sum(
        jnp.dot((e * share).astype(BF16), ref[:, HEAD:], preferred_element_type=F32)
        for e, ref in zip(expo, refs)
    ).astype(BF16)

    @pl.when(i == me)
    def _():
        ox_ref[...] = out

    @pl.when(i != me)
    def _():
        oy_ref[...] = out


def attend(me, flags, query, *keys):
    slabs, count, _ = query.shape
    scalar = pl.BlockSpec(memory_space=pltpu.SMEM)
    out = pl.BlockSpec((count, HEAD), lambda i: (0, 0))
    return pl.pallas_call(
        attend_kernel,
        grid=(slabs,),
        in_specs=[scalar] * 3
        + [pl.BlockSpec((1, count, HEAD), lambda i: (i, 0, 0))]
        + [pl.BlockSpec(k.shape, lambda i: (0, 0)) for k in keys],
        out_specs=[out, out],
        out_shape=[jax.ShapeDtypeStruct((count, HEAD), BF16)] * 2,
        scratch_shapes=[pltpu.VMEM((3 * count, 2 * HEAD), BF16)],
        compiler_params=pltpu.CompilerParams(vmem_limit_bytes=24 << 20),
        name="attend",
    )(me, *flags, query, *keys)


def mix_kernel(ax_ref, ay_ref, wx_ref, wy_ref, o_ref):
    parts, _, width = o_ref.shape
    a = jnp.concatenate([ax_ref[...], ay_ref[...]], axis=1)
    for i in range(parts):
        lines = pl.ds(i * width, width)
        w = jnp.concatenate([wx_ref[lines], wy_ref[lines]], axis=1)
        o_ref[i] = lax.dot_general(a, w, NT, preferred_element_type=F32).astype(BF16)


def mix(attended, panels, parts):
    count = attended[0].shape[0]
    width = panels[0].shape[0] // parts
    return pl.pallas_call(
        mix_kernel,
        out_shape=jax.ShapeDtypeStruct((parts, count, width), BF16),
        compiler_params=pltpu.CompilerParams(vmem_limit_bytes=12 << 20),
        name="mix",
    )(*attended, *panels)


def local(image_tokens, style_tokens, qkv_weight, out_weight, query_gain, key_gain, attend_flags):
    parts = lax.axis_size(TP)
    cores = lax.axis_size("core")
    halves = lax.axis_size("x_hi")
    rows = lax.axis_size(Z)
    depth = qkv_weight.shape[1]

    def swap(block):
        return lax.ppermute(block, "core", [(0, 1), (1, 0)])

    me = lax.axis_index("core").reshape(1)
    mine = pack(qkv_weight, out_weight.T, halves)
    plane = lax.all_to_all(mine, ("x_hi", "core"), 0, 0, tiled=True)
    plane = plane.reshape(halves, cores * depth, 4 * HEAD)
    panel = lax.all_gather(plane, Z, axis=1, tiled=True).reshape(-1, 4 * HEAD)

    image_tokens, style_tokens, attend_flags, _ = lax.optimization_barrier(
        (image_tokens, style_tokens, attend_flags, plane)
    )
    own = spread(image_tokens, TP)
    slabs = (own, swap(own))
    style = spread(style_tokens, "z_hi").reshape(-1, style_tokens.shape[1])
    style = spread(style, ("x_hi",) + TP)
    style = style.reshape((halves, parts) + style.shape[1:])
    styles = (style, swap(style))
    flags = (attend_flags, swap(attend_flags))
    slabs, styles, flags = lax.optimization_barrier((slabs, styles, flags))

    forward, backward, low, high, query = project(
        me, slabs, styles, panel, query_gain.reshape(1, HEAD), key_gain.reshape(1, HEAD)
    )
    chips = halves * rows

    def shift(block, axes, count, by):
        return lax.ppermute(block, axes, [(i, (i + by) % count) for i in range(count)])

    before = shift(forward, ("x_hi",) + Z, chips, 1)
    after = shift(backward, ("x_hi",) + Z, chips, -1)
    low = shift(low, Z, rows, 2)
    high = shift(high, Z, rows, -2)
    panel, query = lax.optimization_barrier((panel, query))
    out_own = panel[:, 3 * HEAD :]
    out_other = swap(out_own)

    ax, ay = attend(me, flags, query, forward, backward, before, after, low, high)
    shares = mix((ax, swap(ay)), (out_own, out_other), parts)
    shares = lax.all_to_all(shares, TP, 0, 0, tiled=True)
    return jnp.sum(shares.astype(F32), axis=0).astype(BF16)


def solution(mesh):
    fine = Mesh(mesh.devices.reshape(2, 4, 4, 2, 4, 2), AXES)
    in_specs = (
        P(LON, TP),
        P(LON, TP),
        P(None, LON, TP),
        P(TP, LON),
        P(),
        P(),
        P(LON, None),
    )
    return jax.shard_map(
        local, mesh=fine, in_specs=in_specs, out_specs=P(LON, TP), check_vma=False
    )
```

```python
import functools
import math

import jax
import jax.numpy as jnp
from jax import lax
from jax.experimental import pallas as pl
from jax.experimental.pallas import tpu as pltpu
from jax.sharding import Mesh, PartitionSpec as P


HEAD = 128
AXES = ("x_hi", "z_hi", "z_lo", "core", "y", "x_lo")
Z = ("z_hi", "z_lo")
LON = ("x_hi",) + Z + ("core",)
TP = ("y", "x_lo")
F32 = jnp.float32
BF16 = jnp.bfloat16


def spread(block, axes):
    count = lax.axis_size(axes)
    return lax.all_to_all(
        jnp.broadcast_to(block[None], (count,) + block.shape), axes, 0, 0, tiled=True
    )


def unit(values, gain):
    return values * lax.rsqrt(jnp.mean(values * values, axis=-1, keepdims=True) + 1e-06) * gain


def pack_kernel(w_ref, o_ref, out_ref):
    copies = out_ref.shape[0] * HEAD // w_ref.shape[2]
    for c in range(w_ref.shape[2] // HEAD):
        lanes = pl.ds(c * HEAD, HEAD)
        row = jnp.concatenate(
            [w_ref[1, :, lanes], w_ref[2, :, lanes], w_ref[0, :, lanes], o_ref[:, lanes]], axis=1
        )
        for r in range(copies):
            out_ref[r * (w_ref.shape[2] // HEAD) + c] = row


def pack(w, o, copies):
    heads = w.shape[2] // HEAD
    return pl.pallas_call(
        pack_kernel,
        out_shape=jax.ShapeDtypeStruct((copies * heads, w.shape[1], 4 * HEAD), BF16),
        name="pack",
    )(w, o)


def project_kernel(
    me_ref,
    x_ref,
    y_ref,
    sx_ref,
    sy_ref,
    w_ref,
    qg_ref,
    kg_ref,
    forward_ref,
    backward_ref,
    low_ref,
    high_ref,
    q_ref,
    acc,
    qacc,
    weights,
    arrived,
):
    step = pl.program_id(0)
    pieces, count, width = x_ref.shape
    groups, _, rows, _ = sx_ref.shape

    def fetch(i):
        lines = pl.ds(i * pieces * width, pieces * width)
        return pltpu.make_async_copy(
            w_ref.at[lines, pl.ds(0, 3 * HEAD)], weights.at[i], arrived.at[i]
        )

    @pl.when(step == 0)
    def _():
        for i in range(weights.shape[0]):
            fetch(i).start()
        acc[...] = jnp.zeros_like(acc)
        qacc[...] = jnp.zeros_like(qacc)

    fetch(step).wait()
    w = weights[step]
    tokens = [(t_ref, ()) for t_ref in (x_ref, y_ref)]
    tokens += [(s_ref, (g,)) for s_ref in (sx_ref, sy_ref) for g in range(groups)]
    t = jnp.concatenate(
        [jnp.concatenate([r[i + (j,)] for j in range(pieces)], axis=1) for r, i in tokens], axis=0
    )
    acc[...] += jnp.dot(t, w[:, : 2 * HEAD], preferred_element_type=F32)
    qacc[...] += jnp.dot(t[: 2 * count], w[:, 2 * HEAD :], preferred_element_type=F32)

    @pl.when(step == pl.num_programs(0) - 1)
    def _():
        kg, qg = kg_ref[...], qg_ref[...]
        far = 2 * groups * rows
        for half, part_ref in enumerate((low_ref, high_ref)):
            lines = pl.ds(half * far // 2, far // 2)
            source = pl.ds(2 * count + half * far // 2, far // 2)
            k = unit(acc[source, :HEAD], kg).astype(BF16)
            v = acc[source, HEAD:].astype(BF16)
            for out_ref in (forward_ref, backward_ref):
                out_ref[lines, :HEAD] = k
                out_ref[lines, HEAD:] = v
            part_ref[:, :HEAD] = k
            part_ref[:, HEAD:] = v
        me = me_ref[0]
        lines = pl.ds(far, count)
        for slab, out_ref in enumerate((backward_ref, forward_ref)):
            mine = pl.ds(pl.multiple_of((slab ^ me) * count, count), count)
            out_ref[lines, :HEAD] = unit(acc[mine, :HEAD], kg).astype(BF16)
            out_ref[lines, HEAD:] = acc[mine, HEAD:].astype(BF16)
            q_ref[slab] = unit(qacc[mine], qg).astype(BF16)


def project(me, slabs, styles, w, query_gain, key_gain):
    parts, count, width = slabs[0].shape
    groups, _, rows, _ = styles[0].shape
    pieces = 2
    far = 2 * groups * rows
    slab = pl.BlockSpec((pieces, count, width), lambda i: (i, 0, 0))
    style = pl.BlockSpec((groups, pieces, rows, width), lambda i: (0, i, 0, 0))
    gain = pl.BlockSpec((1, HEAD), lambda i: (0, 0))

    def out(*shape):
        spec = pl.BlockSpec(shape, lambda i: (0,) * len(shape))
        return spec, jax.ShapeDtypeStruct(shape, BF16)

    pair = (far + count, 2 * HEAD)
    part = (far // 2, 2 * HEAD)
    outs = [out(*pair), out(*pair), out(*part), out(*part), out(2, count, HEAD)]
    return pl.pallas_call(
        project_kernel,
        grid=(parts // pieces,),
        in_specs=[
            pl.BlockSpec(memory_space=pltpu.SMEM),
            slab,
            slab,
            style,
            style,
            pl.BlockSpec(memory_space=pltpu.HBM),
            gain,
            gain,
        ],
        out_specs=[o[0] for o in outs],
        out_shape=[o[1] for o in outs],
        scratch_shapes=[
            pltpu.VMEM((2 * count + far, 2 * HEAD), F32),
            pltpu.VMEM((2 * count, HEAD), F32),
            pltpu.VMEM((parts // pieces, pieces * width, 3 * HEAD), BF16),
            pltpu.SemaphoreType.DMA((parts // pieces,)),
        ],
        compiler_params=pltpu.CompilerParams(vmem_limit_bytes=58 << 20),
        name="project",
    )(me, *slabs, *styles, w, query_gain, key_gain)


NT = (((1,), (1,)), ((), ()))


def attend_kernel(
    me_ref,
    fx_ref,
    fy_ref,
    q_ref,
    forward_ref,
    backward_ref,
    before_ref,
    after_ref,
    low_ref,
    high_ref,
    ox_ref,
    oy_ref,
    near,
):
    i = pl.program_id(0)
    me = me_ref[0]
    count = q_ref.shape[1]
    style = forward_ref.shape[0] - count
    slab = pl.ds(style, count)

    @pl.when(i == 0)
    def _():
        near[pl.ds(0, count)] = backward_ref[slab]
        near[pl.ds(count, count)] = forward_ref[slab]
        near[pl.ds(2 * count, count)] = before_ref[slab]

    @pl.when(i == 1)
    def _():
        near[pl.ds(2 * count, count)] = after_ref[slab]

    flag = jnp.where(i == me, fx_ref[0, 0], fy_ref[0, 0])
    scale = 1.0 / math.sqrt(HEAD)
    q = q_ref[0]
    lines = pl.ds(0, style)
    refs = [near, *(r.at[lines] for r in (forward_ref, before_ref, after_ref)), low_ref, high_ref]
    scores = []
    for n, ref in enumerate(refs):
        part = lax.dot_general(q, ref[:, :HEAD], NT, preferred_element_type=F32) * scale
        scores.append(jnp.where(flag > 0, part, -1e30) if n else part)
    peak = functools.reduce(jnp.maximum, [jnp.max(s, axis=-1, keepdims=True) for s in scores])
    expo = [jnp.exp(s - peak) for s in scores]
    share = 1.0 / sum(jnp.sum(e, axis=-1, keepdims=True) for e in expo)
    out = sum(
        jnp.dot((e * share).astype(BF16), ref[:, HEAD:], preferred_element_type=F32)
        for e, ref in zip(expo, refs)
    ).astype(BF16)

    @pl.when(i == me)
    def _():
        ox_ref[...] = out

    @pl.when(i != me)
    def _():
        oy_ref[...] = out


def attend(me, flags, query, *keys):
    slabs, count, _ = query.shape
    scalar = pl.BlockSpec(memory_space=pltpu.SMEM)
    out = pl.BlockSpec((count, HEAD), lambda i: (0, 0))
    return pl.pallas_call(
        attend_kernel,
        grid=(slabs,),
        in_specs=[scalar] * 3
        + [pl.BlockSpec((1, count, HEAD), lambda i: (i, 0, 0))]
        + [pl.BlockSpec(k.shape, lambda i: (0, 0)) for k in keys],
        out_specs=[out, out],
        out_shape=[jax.ShapeDtypeStruct((count, HEAD), BF16)] * 2,
        scratch_shapes=[pltpu.VMEM((3 * count, 2 * HEAD), BF16)],
        compiler_params=pltpu.CompilerParams(vmem_limit_bytes=24 << 20),
        name="attend",
    )(me, *flags, query, *keys)


def mix_kernel(ax_ref, ay_ref, wx_ref, wy_ref, o_ref):
    parts, _, width = o_ref.shape
    a = jnp.concatenate([ax_ref[...], ay_ref[...]], axis=1)
    for i in range(parts):
        lines = pl.ds(i * width, width)
        w = jnp.concatenate([wx_ref[lines], wy_ref[lines]], axis=1)
        o_ref[i] = lax.dot_general(a, w, NT, preferred_element_type=F32).astype(BF16)


def mix(attended, panels, parts):
    count = attended[0].shape[0]
    width = panels[0].shape[0] // parts
    return pl.pallas_call(
        mix_kernel,
        out_shape=jax.ShapeDtypeStruct((parts, count, width), BF16),
        compiler_params=pltpu.CompilerParams(vmem_limit_bytes=12 << 20),
        name="mix",
    )(*attended, *panels)


def local(image_tokens, style_tokens, qkv_weight, out_weight, query_gain, key_gain, attend_flags):
    parts = lax.axis_size(TP)
    cores = lax.axis_size("core")
    halves = lax.axis_size("x_hi")
    rows = lax.axis_size(Z)
    depth = qkv_weight.shape[1]

    def swap(block):
        return lax.ppermute(block, "core", [(0, 1), (1, 0)])

    me = lax.axis_index("core").reshape(1)
    mine = pack(qkv_weight, out_weight.T, halves)
    plane = lax.all_to_all(mine, ("x_hi", "core"), 0, 0, tiled=True)
    plane = plane.reshape(halves, cores * depth, 4 * HEAD)
    panel = lax.all_gather(plane, Z, axis=1, tiled=True).reshape(-1, 4 * HEAD)

    image_tokens, style_tokens, attend_flags, _ = lax.optimization_barrier(
        (image_tokens, style_tokens, attend_flags, plane)
    )

    def shift(block, axes, count, by):
        return lax.ppermute(block, axes, [(i, (i + by) % count) for i in range(count)])

    step = rows // 4
    style = [style_tokens]
    style += [shift(style_tokens, Z, rows, i * step) for i in (1, 2, 3)]
    style = jnp.concatenate(style, axis=0)
    own = spread(image_tokens, TP)
    slabs = (own, swap(own))
    style = spread(style, ("x_hi",) + TP)
    style = style.reshape((halves, parts) + style.shape[1:])
    styles = (style, swap(style))
    flags = (attend_flags, swap(attend_flags))
    slabs, styles, flags = lax.optimization_barrier((slabs, styles, flags))

    forward, backward, low, high, query = project(
        me, slabs, styles, panel, query_gain.reshape(1, HEAD), key_gain.reshape(1, HEAD)
    )
    chips = halves * rows
    before = shift(forward, ("x_hi",) + Z, chips, 1)
    after = shift(backward, ("x_hi",) + Z, chips, -1)
    low = shift(low, Z, rows, 2)
    high = shift(high, Z, rows, -2)
    panel, query = lax.optimization_barrier((panel, query))
    out_own = panel[:, 3 * HEAD :]
    out_other = swap(out_own)

    ax, ay = attend(me, flags, query, forward, backward, before, after, low, high)
    shares = mix((ax, swap(ay)), (out_own, out_other), parts)
    shares = lax.all_to_all(shares, TP, 0, 0, tiled=True)
    return jnp.sum(shares.astype(F32), axis=0).astype(BF16)


def solution(mesh):
    fine = Mesh(mesh.devices.reshape(2, 4, 4, 2, 4, 2), AXES)
    in_specs = (
        P(LON, TP),
        P(LON, TP),
        P(None, LON, TP),
        P(TP, LON),
        P(),
        P(),
        P(LON, None),
    )
    return jax.shard_map(
        local, mesh=fine, in_specs=in_specs, out_specs=P(LON, TP), check_vma=False
    )
```

```python
import functools
import math

import jax
import jax.numpy as jnp
from jax import lax
from jax.experimental import pallas as pl
from jax.experimental.pallas import tpu as pltpu
from jax.sharding import Mesh, PartitionSpec as P


HEAD = 128
AXES = ("x_hi", "z_hi", "z_lo", "core", "y", "x_lo")
Z = ("z_hi", "z_lo")
LON = ("x_hi",) + Z + ("core",)
TP = ("y", "x_lo")
F32 = jnp.float32
BF16 = jnp.bfloat16


def spread(block, axes):
    count = lax.axis_size(axes)
    return lax.all_to_all(
        jnp.broadcast_to(block[None], (count,) + block.shape), axes, 0, 0, tiled=True
    )


def unit(values, gain):
    return values * lax.rsqrt(jnp.mean(values * values, axis=-1, keepdims=True) + 1e-06) * gain


def pack_kernel(w_ref, o_ref, out_ref):
    copies = out_ref.shape[0] * HEAD // w_ref.shape[2]
    for c in range(w_ref.shape[2] // HEAD):
        lanes = pl.ds(c * HEAD, HEAD)
        row = jnp.concatenate(
            [w_ref[1, :, lanes], w_ref[2, :, lanes], w_ref[0, :, lanes], o_ref[:, lanes]], axis=1
        )
        for r in range(copies):
            out_ref[r * (w_ref.shape[2] // HEAD) + c] = row


def pack(w, o, copies):
    heads = w.shape[2] // HEAD
    return pl.pallas_call(
        pack_kernel,
        out_shape=jax.ShapeDtypeStruct((copies * heads, w.shape[1], 4 * HEAD), BF16),
        name="pack",
    )(w, o)


def project_kernel(
    me_ref,
    x_ref,
    y_ref,
    sx_ref,
    sy_ref,
    w_ref,
    qg_ref,
    kg_ref,
    forward_ref,
    backward_ref,
    low_ref,
    high_ref,
    q_ref,
    acc,
    qacc,
    tokens,
    weights,
    arrived,
):
    steps, total, wide = tokens.shape
    _, count, width = x_ref.shape
    groups, _, rows, _ = sx_ref.shape
    pieces = wide // width
    far = total - 2 * count

    def fetches(step):
        sources = [(r, (), count) for r in (x_ref, y_ref)]
        sources += [(r, (g,), rows) for r in (sx_ref, sy_ref) for g in range(groups)]
        found = [(w_ref.at[pl.ds(step * wide, wide), pl.ds(0, 3 * HEAD)], weights.at[step])]
        for j in range(pieces):
            at = 0
            for r, i, n in sources:
                lines, lanes = pl.ds(at, n), pl.ds(j * width, width)
                found.append((r.at[i + (step * pieces + j,)], tokens.at[step, lines, lanes]))
                at += n
        return [
            pltpu.make_async_copy(a, b, arrived.at[step, n]) for n, (a, b) in enumerate(found)
        ]

    for step in range(steps):
        for copy in fetches(step):
            copy.start()
    acc[...] = jnp.zeros_like(acc)
    qacc[...] = jnp.zeros_like(qacc)

    @pl.loop(0, steps)
    def _(step):
        for copy in fetches(step):
            copy.wait()
        w = weights[step]
        acc[...] += jnp.dot(tokens[step], w[:, : 2 * HEAD], preferred_element_type=F32)
        qacc[...] += jnp.dot(
            tokens[step, : 2 * count], w[:, 2 * HEAD :], preferred_element_type=F32
        )

    kg, qg = kg_ref[...], qg_ref[...]
    for half, part_ref in enumerate((low_ref, high_ref)):
        lines = pl.ds(half * far // 2, far // 2)
        source = pl.ds(2 * count + half * far // 2, far // 2)
        k = unit(acc[source, :HEAD], kg).astype(BF16)
        v = acc[source, HEAD:].astype(BF16)
        for out_ref in (forward_ref, backward_ref):
            out_ref[lines, :HEAD] = k
            out_ref[lines, HEAD:] = v
        part_ref[:, :HEAD] = k
        part_ref[:, HEAD:] = v
    me = me_ref[0]
    lines = pl.ds(far, count)
    for slab, out_ref in enumerate((backward_ref, forward_ref)):
        mine = pl.ds(pl.multiple_of((slab ^ me) * count, count), count)
        out_ref[lines, :HEAD] = unit(acc[mine, :HEAD], kg).astype(BF16)
        out_ref[lines, HEAD:] = acc[mine, HEAD:].astype(BF16)
        q_ref[slab] = unit(qacc[mine], qg).astype(BF16)


def project(me, slabs, styles, w, query_gain, key_gain):
    parts, count, width = slabs[0].shape
    groups, _, rows, _ = styles[0].shape
    pieces = 2
    steps = parts // pieces
    far = 2 * groups * rows
    total = 2 * count + far
    shapes = [(far + count, 2 * HEAD)] * 2 + [(far // 2, 2 * HEAD)] * 2 + [(2, count, HEAD)]
    vmem = pl.BlockSpec(memory_space=pltpu.VMEM)
    hbm = pl.BlockSpec(memory_space=pltpu.HBM)
    return pl.pallas_call(
        project_kernel,
        in_specs=[pl.BlockSpec(memory_space=pltpu.SMEM)] + [hbm] * 5 + [vmem] * 2,
        out_specs=[vmem] * len(shapes),
        out_shape=[jax.ShapeDtypeStruct(shape, BF16) for shape in shapes],
        scratch_shapes=[
            pltpu.VMEM((total, 2 * HEAD), F32),
            pltpu.VMEM((2 * count, HEAD), F32),
            pltpu.VMEM((steps, total, pieces * width), BF16),
            pltpu.VMEM((steps, pieces * width, 3 * HEAD), BF16),
            pltpu.SemaphoreType.DMA((steps, 1 + pieces * (2 + 2 * groups))),
        ],
        compiler_params=pltpu.CompilerParams(vmem_limit_bytes=60 << 20),
        name="project",
    )(me, *slabs, *styles, w, query_gain, key_gain)


NT = (((1,), (1,)), ((), ()))


def attend_kernel(
    me_ref,
    fx_ref,
    fy_ref,
    q_ref,
    forward_ref,
    backward_ref,
    before_ref,
    after_ref,
    low_ref,
    high_ref,
    ox_ref,
    oy_ref,
    near,
):
    i = pl.program_id(0)
    me = me_ref[0]
    count = q_ref.shape[1]
    style = forward_ref.shape[0] - count
    slab = pl.ds(style, count)

    @pl.when(i == 0)
    def _():
        near[pl.ds(0, count)] = backward_ref[slab]
        near[pl.ds(count, count)] = forward_ref[slab]
        near[pl.ds(2 * count, count)] = before_ref[slab]

    @pl.when(i == 1)
    def _():
        near[pl.ds(2 * count, count)] = after_ref[slab]

    flag = jnp.where(i == me, fx_ref[0, 0], fy_ref[0, 0])
    scale = 1.0 / math.sqrt(HEAD)
    q = q_ref[0]
    lines = pl.ds(0, style)
    refs = [near, *(r.at[lines] for r in (forward_ref, before_ref, after_ref)), low_ref, high_ref]
    scores = []
    for n, ref in enumerate(refs):
        part = lax.dot_general(q, ref[:, :HEAD], NT, preferred_element_type=F32) * scale
        scores.append(jnp.where(flag > 0, part, -1e30) if n else part)
    peak = functools.reduce(jnp.maximum, [jnp.max(s, axis=-1, keepdims=True) for s in scores])
    expo = [jnp.exp(s - peak) for s in scores]
    share = 1.0 / sum(jnp.sum(e, axis=-1, keepdims=True) for e in expo)
    out = sum(
        jnp.dot((e * share).astype(BF16), ref[:, HEAD:], preferred_element_type=F32)
        for e, ref in zip(expo, refs)
    ).astype(BF16)

    @pl.when(i == me)
    def _():
        ox_ref[...] = out

    @pl.when(i != me)
    def _():
        oy_ref[...] = out


def attend(me, flags, query, *keys):
    slabs, count, _ = query.shape
    scalar = pl.BlockSpec(memory_space=pltpu.SMEM)
    out = pl.BlockSpec((count, HEAD), lambda i: (0, 0))
    return pl.pallas_call(
        attend_kernel,
        grid=(slabs,),
        in_specs=[scalar] * 3
        + [pl.BlockSpec((1, count, HEAD), lambda i: (i, 0, 0))]
        + [pl.BlockSpec(k.shape, lambda i: (0, 0)) for k in keys],
        out_specs=[out, out],
        out_shape=[jax.ShapeDtypeStruct((count, HEAD), BF16)] * 2,
        scratch_shapes=[pltpu.VMEM((3 * count, 2 * HEAD), BF16)],
        compiler_params=pltpu.CompilerParams(vmem_limit_bytes=24 << 20),
        name="attend",
    )(me, *flags, query, *keys)


def mix_kernel(ax_ref, ay_ref, wx_ref, wy_ref, o_ref):
    parts, _, width = o_ref.shape
    a = jnp.concatenate([ax_ref[...], ay_ref[...]], axis=1)
    for i in range(parts):
        lines = pl.ds(i * width, width)
        w = jnp.concatenate([wx_ref[lines], wy_ref[lines]], axis=1)
        o_ref[i] = lax.dot_general(a, w, NT, preferred_element_type=F32).astype(BF16)


def mix(attended, panels, parts):
    count = attended[0].shape[0]
    width = panels[0].shape[0] // parts
    return pl.pallas_call(
        mix_kernel,
        out_shape=jax.ShapeDtypeStruct((parts, count, width), BF16),
        compiler_params=pltpu.CompilerParams(vmem_limit_bytes=12 << 20),
        name="mix",
    )(*attended, *panels)


def local(image_tokens, style_tokens, qkv_weight, out_weight, query_gain, key_gain, attend_flags):
    parts = lax.axis_size(TP)
    cores = lax.axis_size("core")
    halves = lax.axis_size("x_hi")
    rows = lax.axis_size(Z)
    depth = qkv_weight.shape[1]

    def swap(block):
        return lax.ppermute(block, "core", [(0, 1), (1, 0)])

    me = lax.axis_index("core").reshape(1)
    mine = pack(qkv_weight, out_weight.T, halves)
    plane = lax.all_to_all(mine, ("x_hi", "core"), 0, 0, tiled=True)
    plane = plane.reshape(halves, cores * depth, 4 * HEAD)
    panel = lax.all_gather(plane, Z, axis=1, tiled=True).reshape(-1, 4 * HEAD)

    image_tokens, style_tokens, attend_flags, _ = lax.optimization_barrier(
        (image_tokens, style_tokens, attend_flags, plane)
    )

    def shift(block, axes, count, by):
        return lax.ppermute(block, axes, [(i, (i + by) % count) for i in range(count)])

    step = rows // 4
    style = [style_tokens]
    style += [shift(style_tokens, Z, rows, i * step) for i in (1, 2, 3)]
    style = jnp.concatenate(style, axis=0)
    own = spread(image_tokens, TP)
    slabs = (own, swap(own))
    style = spread(style, ("x_hi",) + TP)
    style = style.reshape((halves, parts) + style.shape[1:])
    styles = (style, swap(style))
    flags = (attend_flags, swap(attend_flags))
    slabs, styles, flags = lax.optimization_barrier((slabs, styles, flags))

    forward, backward, low, high, query = project(
        me, slabs, styles, panel, query_gain.reshape(1, HEAD), key_gain.reshape(1, HEAD)
    )
    chips = halves * rows
    before = shift(forward, ("x_hi",) + Z, chips, 1)
    after = shift(backward, ("x_hi",) + Z, chips, -1)
    low = shift(low, Z, rows, 2)
    high = shift(high, Z, rows, -2)
    panel, query = lax.optimization_barrier((panel, query))
    out_own = panel[:, 3 * HEAD :]
    out_other = swap(out_own)

    ax, ay = attend(me, flags, query, forward, backward, before, after, low, high)
    shares = mix((ax, swap(ay)), (out_own, out_other), parts)
    shares = lax.all_to_all(shares, TP, 0, 0, tiled=True)
    return jnp.sum(shares.astype(F32), axis=0).astype(BF16)


def solution(mesh):
    fine = Mesh(mesh.devices.reshape(2, 4, 4, 2, 4, 2), AXES)
    in_specs = (
        P(LON, TP),
        P(LON, TP),
        P(None, LON, TP),
        P(TP, LON),
        P(),
        P(),
        P(LON, None),
    )
    return jax.shard_map(
        local, mesh=fine, in_specs=in_specs, out_specs=P(LON, TP), check_vma=False
    )
```

```python
import functools
import math

import jax
import jax.numpy as jnp
from jax import lax
from jax.experimental import pallas as pl
from jax.experimental.pallas import tpu as pltpu
from jax.sharding import Mesh, PartitionSpec as P


HEAD = 128
AXES = ("x_hi", "z_hi", "z_lo", "core", "y", "x_lo")
Z = ("z_hi", "z_lo")
LON = ("x_hi",) + Z + ("core",)
TP = ("y", "x_lo")
F32 = jnp.float32
BF16 = jnp.bfloat16


def spread(block, axes):
    count = lax.axis_size(axes)
    return lax.all_to_all(
        jnp.broadcast_to(block[None], (count,) + block.shape), axes, 0, 0, tiled=True
    )


def unit(values, gain):
    return values * lax.rsqrt(jnp.mean(values * values, axis=-1, keepdims=True) + 1e-06) * gain


def pack_kernel(w_ref, o_ref, out_ref):
    copies = out_ref.shape[0] * HEAD // w_ref.shape[2]
    for c in range(w_ref.shape[2] // HEAD):
        lanes = pl.ds(c * HEAD, HEAD)
        row = jnp.concatenate(
            [w_ref[1, :, lanes], w_ref[2, :, lanes], w_ref[0, :, lanes], o_ref[:, lanes]], axis=1
        )
        for r in range(copies):
            out_ref[r * (w_ref.shape[2] // HEAD) + c] = row


def pack(w, o, copies):
    heads = w.shape[2] // HEAD
    return pl.pallas_call(
        pack_kernel,
        out_shape=jax.ShapeDtypeStruct((copies * heads, w.shape[1], 4 * HEAD), BF16),
        name="pack",
    )(w, o)


def fetch_all(found, arrived):
    def copies(step):
        return [
            pltpu.make_async_copy(a, b, arrived.at[step, n]) for n, (a, b) in enumerate(found(step))
        ]

    return copies


def gathered(refs, tokens, w_ref, weights, arrived):
    steps, _, wide = tokens.shape
    columns = weights.shape[2]

    def found(step):
        yield w_ref.at[pl.ds(step * wide, wide), pl.ds(0, columns)], weights.at[step]
        at = 0
        for ref, index, rows in refs:
            width = ref.shape[-1]
            for j in range(wide // width):
                lanes = pl.ds(j * width, width)
                source = ref.at[index + (step * (wide // width) + j,)]
                yield source, tokens.at[step, pl.ds(at, rows), lanes]
            at += rows

    copies = fetch_all(found, arrived)
    for step in range(steps):
        for copy in copies(step):
            copy.start()
    return copies


def far_kernel(
    sx_ref, sy_ref, w_ref, kg_ref, low_ref, high_ref, acc, tokens, weights, arrived
):
    steps, total, _ = tokens.shape
    groups, _, rows, _ = sx_ref.shape
    refs = [(r, (g,), rows) for r in (sx_ref, sy_ref) for g in range(groups)]
    copies = gathered(refs, tokens, w_ref, weights, arrived)
    acc[...] = jnp.zeros_like(acc)

    @pl.loop(0, steps)
    def _(step):
        for copy in copies(step):
            copy.wait()
        acc[...] += jnp.dot(tokens[step], weights[step], preferred_element_type=F32)

    kg = kg_ref[...]
    for half, out_ref in enumerate((low_ref, high_ref)):
        lines = pl.ds(half * total // 2, total // 2)
        out_ref[:, :HEAD] = unit(acc[lines, :HEAD], kg).astype(BF16)
        out_ref[:, HEAD:] = acc[lines, HEAD:].astype(BF16)


def near_kernel(
    me_ref,
    x_ref,
    y_ref,
    w_ref,
    qg_ref,
    kg_ref,
    low_ref,
    high_ref,
    forward_ref,
    backward_ref,
    q_ref,
    acc,
    tokens,
    weights,
    arrived,
):
    steps = tokens.shape[0]
    count = q_ref.shape[1]
    half = low_ref.shape[0]
    copies = gathered([(r, (), count) for r in (x_ref, y_ref)], tokens, w_ref, weights, arrived)
    acc[...] = jnp.zeros_like(acc)
    for out_ref in (forward_ref, backward_ref):
        out_ref[pl.ds(0, half)] = low_ref[...]
        out_ref[pl.ds(half, half)] = high_ref[...]

    @pl.loop(0, steps)
    def _(step):
        for copy in copies(step):
            copy.wait()
        acc[...] += jnp.dot(tokens[step], weights[step], preferred_element_type=F32)

    kg, qg = kg_ref[...], qg_ref[...]
    me = me_ref[0]
    lines = pl.ds(2 * half, count)
    for slab, out_ref in enumerate((backward_ref, forward_ref)):
        mine = pl.ds(pl.multiple_of((slab ^ me) * count, count), count)
        out_ref[lines, :HEAD] = unit(acc[mine, :HEAD], kg).astype(BF16)
        out_ref[lines, HEAD:] = acc[mine, HEAD : 2 * HEAD].astype(BF16)
        q_ref[slab] = unit(acc[mine, 2 * HEAD :], qg).astype(BF16)


VMEM = pl.BlockSpec(memory_space=pltpu.VMEM)
HBM = pl.BlockSpec(memory_space=pltpu.HBM)
SMEM = pl.BlockSpec(memory_space=pltpu.SMEM)
STEPS = 4


def scratch(total, depth, columns, copies):
    return [
        pltpu.VMEM((total, columns), F32),
        pltpu.VMEM((STEPS, total, depth // STEPS), BF16),
        pltpu.VMEM((STEPS, depth // STEPS, columns), BF16),
        pltpu.SemaphoreType.DMA((STEPS, copies)),
    ]


def project_far(styles, w, key_gain):
    groups, parts, rows, _ = styles[0].shape
    total = 2 * groups * rows
    shape = jax.ShapeDtypeStruct((total // 2, 2 * HEAD), BF16)
    return pl.pallas_call(
        far_kernel,
        in_specs=[HBM] * 3 + [VMEM],
        out_specs=[VMEM] * 2,
        out_shape=[shape] * 2,
        scratch_shapes=scratch(
            total, w.shape[0], 2 * HEAD, 1 + 2 * groups * (parts // STEPS)
        ),
        compiler_params=pltpu.CompilerParams(vmem_limit_bytes=60 << 20),
        name="project_far",
    )(*styles, w, key_gain)


def project_near(me, slabs, w, query_gain, key_gain, low, high):
    parts, count, _ = slabs[0].shape
    pair = jax.ShapeDtypeStruct((2 * low.shape[0] + count, 2 * HEAD), BF16)
    return pl.pallas_call(
        near_kernel,
        in_specs=[SMEM] + [HBM] * 3 + [VMEM] * 4,
        out_specs=[VMEM] * 3,
        out_shape=[pair, pair, jax.ShapeDtypeStruct((2, count, HEAD), BF16)],
        scratch_shapes=scratch(2 * count, w.shape[0], 3 * HEAD, 1 + 2 * (parts // STEPS)),
        compiler_params=pltpu.CompilerParams(vmem_limit_bytes=60 << 20),
        name="project_near",
    )(me, *slabs, w, query_gain, key_gain, low, high)


NT = (((1,), (1,)), ((), ()))


def attend_kernel(
    turn,
    me_ref,
    flag_ref,
    q_ref,
    forward_ref,
    backward_ref,
    before_ref,
    after_ref,
    low_ref,
    high_ref,
    o_ref,
    near,
):
    slab = me_ref[0] ^ turn
    count = q_ref.shape[1]
    style = forward_ref.shape[0] - count
    lines = pl.ds(style, count)
    near[pl.ds(0, count)] = backward_ref[lines]
    near[pl.ds(count, count)] = forward_ref[lines]

    @pl.when(slab == 0)
    def _():
        near[pl.ds(2 * count, count)] = before_ref[lines]

    @pl.when(slab == 1)
    def _():
        near[pl.ds(2 * count, count)] = after_ref[lines]

    scale = 1.0 / math.sqrt(HEAD)
    q = q_ref[slab]
    lines = pl.ds(0, style)
    refs = [near, *(r.at[lines] for r in (forward_ref, before_ref, after_ref)), low_ref, high_ref]
    scores = []
    for n, ref in enumerate(refs):
        part = lax.dot_general(q, ref[:, :HEAD], NT, preferred_element_type=F32) * scale
        scores.append(jnp.where(flag_ref[0, 0] > 0, part, -1e30) if n else part)
    peak = functools.reduce(jnp.maximum, [jnp.max(s, axis=-1, keepdims=True) for s in scores])
    expo = [jnp.exp(s - peak) for s in scores]
    share = 1.0 / sum(jnp.sum(e, axis=-1, keepdims=True) for e in expo)
    o_ref[...] = sum(
        jnp.dot((e * share).astype(BF16), ref[:, HEAD:], preferred_element_type=F32)
        for e, ref in zip(expo, refs)
    ).astype(BF16)


def attend(turn, me, flag, query, *keys):
    count = query.shape[1]
    scalar = pl.BlockSpec(memory_space=pltpu.SMEM)
    vmem = pl.BlockSpec(memory_space=pltpu.VMEM)
    return pl.pallas_call(
        functools.partial(attend_kernel, turn),
        in_specs=[scalar] * 2 + [vmem] * (1 + len(keys)),
        out_specs=vmem,
        out_shape=jax.ShapeDtypeStruct((count, HEAD), BF16),
        scratch_shapes=[pltpu.VMEM((3 * count, 2 * HEAD), BF16)],
        compiler_params=pltpu.CompilerParams(vmem_limit_bytes=24 << 20),
        cost_estimate=pl.CostEstimate(
            flops=11 * 256 * 256 * 4 * HEAD, bytes_accessed=2 << 20, transcendentals=11 << 16
        ),
    )(me, flag, query, *keys)


def mix_kernel(ax_ref, ay_ref, wx_ref, wy_ref, o_ref):
    parts, _, width = o_ref.shape
    a = jnp.concatenate([ax_ref[...], ay_ref[...]], axis=1)
    for i in range(parts):
        lines = pl.ds(i * width, width)
        w = jnp.concatenate([wx_ref[lines], wy_ref[lines]], axis=1)
        o_ref[i] = lax.dot_general(a, w, NT, preferred_element_type=F32).astype(BF16)


def mix(attended, panels, parts):
    count = attended[0].shape[0]
    width = panels[0].shape[0] // parts
    return pl.pallas_call(
        mix_kernel,
        out_shape=jax.ShapeDtypeStruct((parts, count, width), BF16),
        compiler_params=pltpu.CompilerParams(vmem_limit_bytes=12 << 20),
        name="mix",
    )(*attended, *panels)


def local(image_tokens, style_tokens, qkv_weight, out_weight, query_gain, key_gain, attend_flags):
    parts = lax.axis_size(TP)
    cores = lax.axis_size("core")
    halves = lax.axis_size("x_hi")
    rows = lax.axis_size(Z)
    depth = qkv_weight.shape[1]

    def swap(block):
        return lax.ppermute(block, "core", [(0, 1), (1, 0)])

    me = lax.axis_index("core").reshape(1)
    mine = pack(qkv_weight, out_weight.T, halves)
    plane = lax.all_to_all(mine, ("x_hi", "core"), 0, 0, tiled=True)
    plane = plane.reshape(halves, cores * depth, 4 * HEAD)
    panel = lax.all_gather(plane, Z, axis=1, tiled=True).reshape(-1, 4 * HEAD)

    image_tokens, style_tokens, attend_flags, _ = lax.optimization_barrier(
        (image_tokens, style_tokens, attend_flags, plane)
    )

    def shift(block, axes, count, by):
        return lax.ppermute(block, axes, [(i, (i + by) % count) for i in range(count)])

    step = rows // 4
    style = [style_tokens]
    style += [shift(style_tokens, Z, rows, i * step) for i in (1, 2, 3)]
    style = jnp.concatenate(style, axis=0)
    own = spread(image_tokens, TP)
    slabs = (own, swap(own))
    style = spread(style, ("x_hi",) + TP)
    style = style.reshape((halves, parts) + style.shape[1:])
    styles = (style, swap(style))
    flags = (attend_flags, swap(attend_flags))
    slabs, styles, flags = lax.optimization_barrier((slabs, styles, flags))

    key_gain = key_gain.reshape(1, HEAD)
    low, high = project_far(styles, panel, key_gain)
    forward, backward, query = project_near(
        me, slabs, panel, query_gain.reshape(1, HEAD), key_gain, low, high
    )
    chips = halves * rows
    low = shift(low, Z, rows, 2)
    high = shift(high, Z, rows, -2)
    before = shift(forward, ("x_hi",) + Z, chips, 1)
    after = shift(backward, ("x_hi",) + Z, chips, -1)
    panel, query = lax.optimization_barrier((panel, query))
    out_own = panel[:, 3 * HEAD :]
    out_other = swap(out_own)

    keys = (forward, backward, before, after, low, high)
    theirs = swap(attend(1, me, flags[1], query, *keys))
    mine = attend(0, me, flags[0], query, *keys)
    shares = mix((mine, theirs), (out_own, out_other), parts)
    shares = lax.all_to_all(shares, TP, 0, 0, tiled=True)
    return jnp.sum(shares.astype(F32), axis=0).astype(BF16)


def solution(mesh):
    fine = Mesh(mesh.devices.reshape(2, 4, 4, 2, 4, 2), AXES)
    in_specs = (
        P(LON, TP),
        P(LON, TP),
        P(None, LON, TP),
        P(TP, LON),
        P(),
        P(),
        P(LON, None),
    )
    return jax.shard_map(
        local, mesh=fine, in_specs=in_specs, out_specs=P(LON, TP), check_vma=False
    )
```

```python
import functools
import math

import jax
import jax.numpy as jnp
from jax import lax
from jax.experimental import pallas as pl
from jax.experimental.pallas import tpu as pltpu
from jax.sharding import Mesh, PartitionSpec as P


HEAD = 128
AXES = ("x_hi", "z_hi", "z_lo", "core", "y", "x_lo")
Z = ("z_hi", "z_lo")
LON = ("x_hi",) + Z + ("core",)
TP = ("y", "x_lo")
F32 = jnp.float32
BF16 = jnp.bfloat16


def spread(block, axes):
    count = lax.axis_size(axes)
    return lax.all_to_all(
        jnp.broadcast_to(block[None], (count,) + block.shape), axes, 0, 0, tiled=True
    )


def unit(values, gain):
    return values * lax.rsqrt(jnp.mean(values * values, axis=-1, keepdims=True) + 1e-06) * gain


def pack_kernel(w_ref, o_ref, out_ref):
    copies = out_ref.shape[0] * HEAD // w_ref.shape[2]
    for c in range(w_ref.shape[2] // HEAD):
        lanes = pl.ds(c * HEAD, HEAD)
        row = jnp.concatenate(
            [w_ref[1, :, lanes], w_ref[2, :, lanes], w_ref[0, :, lanes], o_ref[:, lanes]], axis=1
        )
        for r in range(copies):
            out_ref[r * (w_ref.shape[2] // HEAD) + c] = row


def pack(w, o, copies):
    heads = w.shape[2] // HEAD
    return pl.pallas_call(
        pack_kernel,
        out_shape=jax.ShapeDtypeStruct((copies * heads, w.shape[1], 4 * HEAD), BF16),
        name="pack",
    )(w, o)


def project_kernel(
    me_ref,
    x_ref,
    y_ref,
    sx_ref,
    sy_ref,
    w_ref,
    qg_ref,
    kg_ref,
    forward_ref,
    backward_ref,
    low_ref,
    high_ref,
    q_ref,
    acc,
    qacc,
    tokens,
    weights,
    arrived,
):
    steps, total, wide = tokens.shape
    _, count, width = x_ref.shape
    groups, _, rows, _ = sx_ref.shape
    pieces = wide // width
    far = total - 2 * count

    def fetches(step):
        sources = [(r, (), count) for r in (x_ref, y_ref)]
        sources += [(r, (g,), rows) for r in (sx_ref, sy_ref) for g in range(groups)]
        found = [(w_ref.at[pl.ds(step * wide, wide), pl.ds(0, 3 * HEAD)], weights.at[step])]
        for j in range(pieces):
            at = 0
            for r, i, n in sources:
                lines, lanes = pl.ds(at, n), pl.ds(j * width, width)
                found.append((r.at[i + (step * pieces + j,)], tokens.at[step, lines, lanes]))
                at += n
        return [
            pltpu.make_async_copy(a, b, arrived.at[step, n]) for n, (a, b) in enumerate(found)
        ]

    for step in range(steps):
        for copy in fetches(step):
            copy.start()
    acc[...] = jnp.zeros_like(acc)
    qacc[...] = jnp.zeros_like(qacc)

    @pl.loop(0, steps)
    def _(step):
        for copy in fetches(step):
            copy.wait()
        w = weights[step]
        acc[...] += jnp.dot(tokens[step], w[:, : 2 * HEAD], preferred_element_type=F32)
        qacc[...] += jnp.dot(
            tokens[step, : 2 * count], w[:, 2 * HEAD :], preferred_element_type=F32
        )

    kg, qg = kg_ref[...], qg_ref[...]
    for half, part_ref in enumerate((low_ref, high_ref)):
        lines = pl.ds(half * far // 2, far // 2)
        source = pl.ds(2 * count + half * far // 2, far // 2)
        k = unit(acc[source, :HEAD], kg).astype(BF16)
        v = acc[source, HEAD:].astype(BF16)
        for out_ref in (forward_ref, backward_ref):
            out_ref[lines, :HEAD] = k
            out_ref[lines, HEAD:] = v
        part_ref[:, :HEAD] = k
        part_ref[:, HEAD:] = v
    me = me_ref[0]
    lines = pl.ds(far, count)
    for slab, out_ref in enumerate((backward_ref, forward_ref)):
        mine = pl.ds(pl.multiple_of((slab ^ me) * count, count), count)
        out_ref[lines, :HEAD] = unit(acc[mine, :HEAD], kg).astype(BF16)
        out_ref[lines, HEAD:] = acc[mine, HEAD:].astype(BF16)
        q_ref[slab] = unit(qacc[mine], qg).astype(BF16)


def project(me, slabs, styles, w, query_gain, key_gain):
    parts, count, width = slabs[0].shape
    groups, _, rows, _ = styles[0].shape
    pieces = 2
    steps = parts // pieces
    far = 2 * groups * rows
    total = 2 * count + far
    shapes = [(far + count, 2 * HEAD)] * 2 + [(far // 2, 2 * HEAD)] * 2 + [(2, count, HEAD)]
    vmem = pl.BlockSpec(memory_space=pltpu.VMEM)
    hbm = pl.BlockSpec(memory_space=pltpu.HBM)
    return pl.pallas_call(
        project_kernel,
        in_specs=[pl.BlockSpec(memory_space=pltpu.SMEM)] + [hbm] * 5 + [vmem] * 2,
        out_specs=[vmem] * len(shapes),
        out_shape=[jax.ShapeDtypeStruct(shape, BF16) for shape in shapes],
        scratch_shapes=[
            pltpu.VMEM((total, 2 * HEAD), F32),
            pltpu.VMEM((2 * count, HEAD), F32),
            pltpu.VMEM((steps, total, pieces * width), BF16),
            pltpu.VMEM((steps, pieces * width, 3 * HEAD), BF16),
            pltpu.SemaphoreType.DMA((steps, 1 + pieces * (2 + 2 * groups))),
        ],
        compiler_params=pltpu.CompilerParams(vmem_limit_bytes=60 << 20),
        name="project",
    )(me, *slabs, *styles, w, query_gain, key_gain)


NT = (((1,), (1,)), ((), ()))


def attend_kernel(
    turn,
    me_ref,
    flag_ref,
    q_ref,
    forward_ref,
    backward_ref,
    before_ref,
    after_ref,
    low_ref,
    high_ref,
    o_ref,
    near,
):
    slab = me_ref[0] ^ turn
    count = q_ref.shape[1]
    style = forward_ref.shape[0] - count
    lines = pl.ds(style, count)
    near[pl.ds(0, count)] = backward_ref[lines]
    near[pl.ds(count, count)] = forward_ref[lines]

    @pl.when(slab == 0)
    def _():
        near[pl.ds(2 * count, count)] = before_ref[lines]

    @pl.when(slab == 1)
    def _():
        near[pl.ds(2 * count, count)] = after_ref[lines]

    scale = 1.0 / math.sqrt(HEAD)
    q = q_ref[slab]
    lines = pl.ds(0, style)
    refs = [near, *(r.at[lines] for r in (forward_ref, before_ref, after_ref)), low_ref, high_ref]
    scores = []
    for n, ref in enumerate(refs):
        part = lax.dot_general(q, ref[:, :HEAD], NT, preferred_element_type=F32) * scale
        scores.append(jnp.where(flag_ref[0, 0] > 0, part, -1e30) if n else part)
    peak = functools.reduce(jnp.maximum, [jnp.max(s, axis=-1, keepdims=True) for s in scores])
    expo = [jnp.exp(s - peak) for s in scores]
    share = 1.0 / sum(jnp.sum(e, axis=-1, keepdims=True) for e in expo)
    o_ref[...] = sum(
        jnp.dot((e * share).astype(BF16), ref[:, HEAD:], preferred_element_type=F32)
        for e, ref in zip(expo, refs)
    ).astype(BF16)


def attend(turn, me, flag, query, *keys):
    count = query.shape[1]
    scalar = pl.BlockSpec(memory_space=pltpu.SMEM)
    vmem = pl.BlockSpec(memory_space=pltpu.VMEM)
    return pl.pallas_call(
        functools.partial(attend_kernel, turn),
        in_specs=[scalar] * 2 + [vmem] * (1 + len(keys)),
        out_specs=vmem,
        out_shape=jax.ShapeDtypeStruct((count, HEAD), BF16),
        scratch_shapes=[pltpu.VMEM((3 * count, 2 * HEAD), BF16)],
        compiler_params=pltpu.CompilerParams(vmem_limit_bytes=24 << 20),
        cost_estimate=pl.CostEstimate(
            flops=11 * 256 * 256 * 4 * HEAD, bytes_accessed=2 << 20, transcendentals=11 << 16
        ),
    )(me, flag, query, *keys)


def mix_kernel(ax_ref, ay_ref, wx_ref, wy_ref, o_ref):
    parts, _, width = o_ref.shape
    a = jnp.concatenate([ax_ref[...], ay_ref[...]], axis=1)
    for i in range(parts):
        lines = pl.ds(i * width, width)
        w = jnp.concatenate([wx_ref[lines], wy_ref[lines]], axis=1)
        o_ref[i] = lax.dot_general(a, w, NT, preferred_element_type=F32).astype(BF16)


def mix(attended, panels, parts):
    count = attended[0].shape[0]
    width = panels[0].shape[0] // parts
    return pl.pallas_call(
        mix_kernel,
        out_shape=jax.ShapeDtypeStruct((parts, count, width), BF16),
        compiler_params=pltpu.CompilerParams(vmem_limit_bytes=12 << 20),
        name="mix",
    )(*attended, *panels)


def local(image_tokens, style_tokens, qkv_weight, out_weight, query_gain, key_gain, attend_flags):
    parts = lax.axis_size(TP)
    cores = lax.axis_size("core")
    halves = lax.axis_size("x_hi")
    rows = lax.axis_size(Z)
    depth = qkv_weight.shape[1]

    def swap(block):
        return lax.ppermute(block, "core", [(0, 1), (1, 0)])

    me = lax.axis_index("core").reshape(1)
    mine = pack(qkv_weight, out_weight.T, halves)
    plane = lax.all_to_all(mine, ("x_hi", "core"), 0, 0, tiled=True)
    plane = plane.reshape(halves, cores * depth, 4 * HEAD)
    panel = lax.all_gather(plane, Z, axis=1, tiled=True).reshape(-1, 4 * HEAD)

    image_tokens, style_tokens, attend_flags, _ = lax.optimization_barrier(
        (image_tokens, style_tokens, attend_flags, plane)
    )

    def shift(block, axes, count, by):
        return lax.ppermute(block, axes, [(i, (i + by) % count) for i in range(count)])

    step = rows // 4
    style = [style_tokens]
    style += [shift(style_tokens, Z, rows, i * step) for i in (1, 2, 3)]
    style = jnp.concatenate(style, axis=0)
    own = spread(image_tokens, TP)
    slabs = (own, swap(own))
    style = spread(style, ("x_hi",) + TP)
    style = style.reshape((halves, parts) + style.shape[1:])
    styles = (style, swap(style))
    flags = (attend_flags, swap(attend_flags))
    slabs, styles, flags = lax.optimization_barrier((slabs, styles, flags))

    forward, backward, low, high, query = project(
        me, slabs, styles, panel, query_gain.reshape(1, HEAD), key_gain.reshape(1, HEAD)
    )
    chips = halves * rows
    before = shift(forward, ("x_hi",) + Z, chips, 1)
    after = shift(backward, ("x_hi",) + Z, chips, -1)
    low = shift(low, Z, rows, 2)
    high = shift(high, Z, rows, -2)
    panel, query = lax.optimization_barrier((panel, query))
    out_own = panel[:, 3 * HEAD :]
    out_other = swap(out_own)

    keys = (forward, backward, before, after, low, high)
    theirs = swap(attend(1, me, flags[1], query, *keys))
    mine = attend(0, me, flags[0], query, *keys)
    shares = mix((mine, theirs), (out_own, out_other), parts)
    shares = lax.all_to_all(shares, TP, 0, 0, tiled=True)
    return jnp.sum(shares.astype(F32), axis=0).astype(BF16)


def solution(mesh):
    fine = Mesh(mesh.devices.reshape(2, 4, 4, 2, 4, 2), AXES)
    in_specs = (
        P(LON, TP),
        P(LON, TP),
        P(None, LON, TP),
        P(TP, LON),
        P(),
        P(),
        P(LON, None),
    )
    return jax.shard_map(
        local, mesh=fine, in_specs=in_specs, out_specs=P(LON, TP), check_vma=False
    )
```

```python
import functools
import math

import jax
import jax.numpy as jnp
from jax import lax
from jax.experimental import pallas as pl
from jax.experimental.pallas import tpu as pltpu
from jax.sharding import Mesh, PartitionSpec as P


HEAD = 128
AXES = ("x_hi", "z_hi", "z_lo", "core", "y", "x_lo")
Z = ("z_hi", "z_lo")
LON = ("x_hi",) + Z + ("core",)
TP = ("y", "x_lo")
F32 = jnp.float32
BF16 = jnp.bfloat16


def spread(block, axes):
    count = lax.axis_size(axes)
    return lax.all_to_all(
        jnp.broadcast_to(block[None], (count,) + block.shape), axes, 0, 0, tiled=True
    )


def unit(values, gain):
    return values * lax.rsqrt(jnp.mean(values * values, axis=-1, keepdims=True) + 1e-06) * gain


def pack_kernel(w_ref, o_ref, out_ref):
    copies = out_ref.shape[0] * HEAD // w_ref.shape[2]
    for c in range(w_ref.shape[2] // HEAD):
        lanes = pl.ds(c * HEAD, HEAD)
        row = jnp.concatenate(
            [w_ref[1, :, lanes], w_ref[2, :, lanes], w_ref[0, :, lanes], o_ref[:, lanes]], axis=1
        )
        for r in range(copies):
            out_ref[r * (w_ref.shape[2] // HEAD) + c] = row


def pack(w, o, copies):
    heads = w.shape[2] // HEAD
    return pl.pallas_call(
        pack_kernel,
        out_shape=jax.ShapeDtypeStruct((copies * heads, w.shape[1], 4 * HEAD), BF16),
        name="pack",
    )(w, o)


def project_kernel(
    me_ref,
    x_ref,
    y_ref,
    sx_ref,
    sy_ref,
    w_ref,
    qg_ref,
    kg_ref,
    forward_ref,
    backward_ref,
    far_ref,
    q_ref,
    acc,
    qacc,
    tokens,
    weights,
    arrived,
):
    steps, total, wide = tokens.shape
    _, count, width = x_ref.shape
    groups, _, rows, _ = sx_ref.shape
    pieces = wide // width
    far = total - 2 * count

    def fetches(step):
        sources = [(r, (), count) for r in (x_ref, y_ref)]
        sources += [(r, (g,), rows) for r in (sx_ref, sy_ref) for g in range(groups)]
        found = [(w_ref.at[pl.ds(step * wide, wide), pl.ds(0, 3 * HEAD)], weights.at[step])]
        for j in range(pieces):
            at = 0
            for r, i, n in sources:
                lines, lanes = pl.ds(at, n), pl.ds(j * width, width)
                found.append((r.at[i + (step * pieces + j,)], tokens.at[step, lines, lanes]))
                at += n
        return [
            pltpu.make_async_copy(a, b, arrived.at[step, n]) for n, (a, b) in enumerate(found)
        ]

    for step in range(steps):
        for copy in fetches(step):
            copy.start()
    acc[...] = jnp.zeros_like(acc)
    qacc[...] = jnp.zeros_like(qacc)

    @pl.loop(0, steps)
    def _(step):
        for copy in fetches(step):
            copy.wait()
        w = weights[step]
        acc[...] += jnp.dot(tokens[step], w[:, : 2 * HEAD], preferred_element_type=F32)
        qacc[...] += jnp.dot(
            tokens[step, : 2 * count], w[:, 2 * HEAD :], preferred_element_type=F32
        )

    kg, qg = kg_ref[...], qg_ref[...]
    k = unit(acc[pl.ds(2 * count, far), :HEAD], kg).astype(BF16)
    v = acc[pl.ds(2 * count, far), HEAD:].astype(BF16)
    for out_ref in (forward_ref, backward_ref, far_ref):
        out_ref[pl.ds(0, far), :HEAD] = k
        out_ref[pl.ds(0, far), HEAD:] = v
    me = me_ref[0]
    lines = pl.ds(far, count)
    for slab, out_ref in enumerate((backward_ref, forward_ref)):
        mine = pl.ds(pl.multiple_of((slab ^ me) * count, count), count)
        out_ref[lines, :HEAD] = unit(acc[mine, :HEAD], kg).astype(BF16)
        out_ref[lines, HEAD:] = acc[mine, HEAD:].astype(BF16)
        q_ref[slab] = unit(qacc[mine], qg).astype(BF16)


def project(me, slabs, styles, w, query_gain, key_gain):
    parts, count, width = slabs[0].shape
    groups, _, rows, _ = styles[0].shape
    pieces = 2
    steps = parts // pieces
    far = 2 * groups * rows
    total = 2 * count + far
    shapes = [(far + count, 2 * HEAD)] * 2 + [(far, 2 * HEAD), (2, count, HEAD)]
    vmem = pl.BlockSpec(memory_space=pltpu.VMEM)
    hbm = pl.BlockSpec(memory_space=pltpu.HBM)
    return pl.pallas_call(
        project_kernel,
        in_specs=[pl.BlockSpec(memory_space=pltpu.SMEM)] + [hbm] * 5 + [vmem] * 2,
        out_specs=[vmem] * len(shapes),
        out_shape=[jax.ShapeDtypeStruct(shape, BF16) for shape in shapes],
        scratch_shapes=[
            pltpu.VMEM((total, 2 * HEAD), F32),
            pltpu.VMEM((2 * count, HEAD), F32),
            pltpu.VMEM((steps, total, pieces * width), BF16),
            pltpu.VMEM((steps, pieces * width, 3 * HEAD), BF16),
            pltpu.SemaphoreType.DMA((steps, 1 + pieces * (2 + 2 * groups))),
        ],
        compiler_params=pltpu.CompilerParams(vmem_limit_bytes=60 << 20),
        name="project",
    )(me, *slabs, *styles, w, query_gain, key_gain)


NT = (((1,), (1,)), ((), ()))


def attend_kernel(
    turn,
    me_ref,
    flag_ref,
    q_ref,
    forward_ref,
    backward_ref,
    before_ref,
    after_ref,
    far_ref,
    o_ref,
    near,
):
    slab = me_ref[0] ^ turn
    count = q_ref.shape[1]
    style = forward_ref.shape[0] - count
    lines = pl.ds(style, count)
    near[pl.ds(0, count)] = backward_ref[lines]
    near[pl.ds(count, count)] = forward_ref[lines]

    @pl.when(slab == 0)
    def _():
        near[pl.ds(2 * count, count)] = before_ref[lines]

    @pl.when(slab == 1)
    def _():
        near[pl.ds(2 * count, count)] = after_ref[lines]

    scale = 1.0 / math.sqrt(HEAD)
    q = q_ref[slab]
    lines = pl.ds(0, style)
    refs = [near, *(r.at[lines] for r in (forward_ref, before_ref, after_ref)), far_ref]
    scores = []
    for n, ref in enumerate(refs):
        part = lax.dot_general(q, ref[:, :HEAD], NT, preferred_element_type=F32) * scale
        scores.append(jnp.where(flag_ref[0, 0] > 0, part, -1e30) if n else part)
    peak = functools.reduce(jnp.maximum, [jnp.max(s, axis=-1, keepdims=True) for s in scores])
    expo = [jnp.exp(s - peak) for s in scores]
    share = 1.0 / sum(jnp.sum(e, axis=-1, keepdims=True) for e in expo)
    o_ref[...] = sum(
        jnp.dot((e * share).astype(BF16), ref[:, HEAD:], preferred_element_type=F32)
        for e, ref in zip(expo, refs)
    ).astype(BF16)


def attend(turn, me, flag, query, *keys):
    count = query.shape[1]
    scalar = pl.BlockSpec(memory_space=pltpu.SMEM)
    vmem = pl.BlockSpec(memory_space=pltpu.VMEM)
    return pl.pallas_call(
        functools.partial(attend_kernel, turn),
        in_specs=[scalar] * 2 + [vmem] * (1 + len(keys)),
        out_specs=vmem,
        out_shape=jax.ShapeDtypeStruct((count, HEAD), BF16),
        scratch_shapes=[pltpu.VMEM((3 * count, 2 * HEAD), BF16)],
        compiler_params=pltpu.CompilerParams(vmem_limit_bytes=24 << 20),
        cost_estimate=pl.CostEstimate(
            flops=11 * 256 * 256 * 4 * HEAD, bytes_accessed=2 << 20, transcendentals=11 << 16
        ),
    )(me, flag, query, *keys)


def mix_kernel(ax_ref, ay_ref, wx_ref, wy_ref, o_ref):
    parts, _, width = o_ref.shape
    a = jnp.concatenate([ax_ref[...], ay_ref[...]], axis=1)
    for i in range(parts):
        lines = pl.ds(i * width, width)
        w = jnp.concatenate([wx_ref[lines], wy_ref[lines]], axis=1)
        o_ref[i] = lax.dot_general(a, w, NT, preferred_element_type=F32).astype(BF16)


def mix(attended, panels, parts):
    count = attended[0].shape[0]
    width = panels[0].shape[0] // parts
    return pl.pallas_call(
        mix_kernel,
        out_shape=jax.ShapeDtypeStruct((parts, count, width), BF16),
        compiler_params=pltpu.CompilerParams(vmem_limit_bytes=12 << 20),
        name="mix",
    )(*attended, *panels)


def local(image_tokens, style_tokens, qkv_weight, out_weight, query_gain, key_gain, attend_flags):
    parts = lax.axis_size(TP)
    cores = lax.axis_size("core")
    halves = lax.axis_size("x_hi")
    rows = lax.axis_size(Z)
    depth = qkv_weight.shape[1]

    def swap(block):
        return lax.ppermute(block, "core", [(0, 1), (1, 0)])

    me = lax.axis_index("core").reshape(1)
    mine = pack(qkv_weight, out_weight.T, halves)
    plane = lax.all_to_all(mine, ("x_hi", "core"), 0, 0, tiled=True)
    plane = plane.reshape(halves, cores * depth, 4 * HEAD)
    panel = lax.all_gather(plane, Z, axis=1, tiled=True).reshape(-1, 4 * HEAD)

    image_tokens, style_tokens, attend_flags, _ = lax.optimization_barrier(
        (image_tokens, style_tokens, attend_flags, plane)
    )

    def shift(block, axes, count, by):
        return lax.ppermute(block, axes, [(i, (i + by) % count) for i in range(count)])

    step = rows // 4
    style = [style_tokens]
    style += [shift(style_tokens, Z, rows, i * step) for i in (1, 2, 3)]
    style = jnp.concatenate(style, axis=0)
    own = spread(image_tokens, TP)
    slabs = (own, swap(own))
    style = spread(style, ("x_hi",) + TP)
    style = style.reshape((halves, parts) + style.shape[1:])
    styles = (style, swap(style))
    flags = (attend_flags, swap(attend_flags))
    slabs, styles, flags = lax.optimization_barrier((slabs, styles, flags))

    forward, backward, far, query = project(
        me, slabs, styles, panel, query_gain.reshape(1, HEAD), key_gain.reshape(1, HEAD)
    )
    chips = halves * rows
    before = shift(forward, ("x_hi",) + Z, chips, 1)
    after = shift(backward, ("x_hi",) + Z, chips, -1)
    pairs = [
        (i * cores + c, (i + 2 - 4 * c) % rows * cores + c) for i in range(rows) for c in (0, 1)
    ]
    far = lax.ppermute(far, Z + ("core",), pairs)
    panel, query = lax.optimization_barrier((panel, query))
    out_own = panel[:, 3 * HEAD :]
    out_other = swap(out_own)

    keys = (forward, backward, before, after, far)
    theirs = swap(attend(1, me, flags[1], query, *keys))
    mine = attend(0, me, flags[0], query, *keys)
    shares = mix((mine, theirs), (out_own, out_other), parts)
    shares = lax.all_to_all(shares, TP, 0, 0, tiled=True)
    return jnp.sum(shares.astype(F32), axis=0).astype(BF16)


def solution(mesh):
    fine = Mesh(mesh.devices.reshape(2, 4, 4, 2, 4, 2), AXES)
    in_specs = (
        P(LON, TP),
        P(LON, TP),
        P(None, LON, TP),
        P(TP, LON),
        P(),
        P(),
        P(LON, None),
    )
    return jax.shard_map(
        local, mesh=fine, in_specs=in_specs, out_specs=P(LON, TP), check_vma=False
    )
```

```python
import functools
import math

import jax
import jax.numpy as jnp
from jax import lax
from jax.experimental import pallas as pl
from jax.experimental.pallas import tpu as pltpu
from jax.sharding import Mesh, PartitionSpec as P


HEAD = 128
AXES = ("x_hi", "z_hi", "z_lo", "core", "y", "x_lo")
Z = ("z_hi", "z_lo")
LON = ("x_hi",) + Z + ("core",)
TP = ("y", "x_lo")
F32 = jnp.float32
BF16 = jnp.bfloat16


def spread(block, axes):
    count = lax.axis_size(axes)
    return lax.all_to_all(
        jnp.broadcast_to(block[None], (count,) + block.shape), axes, 0, 0, tiled=True
    )


def unit(values, gain):
    return values * lax.rsqrt(jnp.mean(values * values, axis=-1, keepdims=True) + 1e-06) * gain


def pack_kernel(w_ref, o_ref, out_ref):
    copies = out_ref.shape[0] * HEAD // w_ref.shape[2]
    for c in range(w_ref.shape[2] // HEAD):
        lanes = pl.ds(c * HEAD, HEAD)
        row = jnp.concatenate(
            [w_ref[1, :, lanes], w_ref[2, :, lanes], w_ref[0, :, lanes], o_ref[:, lanes]], axis=1
        )
        for r in range(copies):
            out_ref[r * (w_ref.shape[2] // HEAD) + c] = row


def pack(w, o, copies):
    heads = w.shape[2] // HEAD
    return pl.pallas_call(
        pack_kernel,
        out_shape=jax.ShapeDtypeStruct((copies * heads, w.shape[1], 4 * HEAD), BF16),
        compiler_params=pltpu.CompilerParams(vmem_limit_bytes=4 << 20),
        name="pack",
    )(w, o)


def project_kernel(
    me_ref,
    x_ref,
    y_ref,
    sx_ref,
    sy_ref,
    w_ref,
    qg_ref,
    kg_ref,
    forward_ref,
    backward_ref,
    far_ref,
    q_ref,
    acc,
    qacc,
    tokens,
    weights,
    arrived,
):
    steps, total, wide = tokens.shape
    _, count, width = x_ref.shape
    groups, _, rows, _ = sx_ref.shape
    pieces = wide // width
    far = total - 2 * count

    def fetches(step):
        sources = [(r, (), count) for r in (x_ref, y_ref)]
        sources += [(r, (g,), rows) for r in (sx_ref, sy_ref) for g in range(groups)]
        found = [(w_ref.at[pl.ds(step * wide, wide), pl.ds(0, 3 * HEAD)], weights.at[step])]
        for j in range(pieces):
            at = 0
            for r, i, n in sources:
                lines, lanes = pl.ds(at, n), pl.ds(j * width, width)
                found.append((r.at[i + (step * pieces + j,)], tokens.at[step, lines, lanes]))
                at += n
        return [
            pltpu.make_async_copy(a, b, arrived.at[step, n]) for n, (a, b) in enumerate(found)
        ]

    for step in range(steps):
        for copy in fetches(step):
            copy.start()
    acc[...] = jnp.zeros_like(acc)
    qacc[...] = jnp.zeros_like(qacc)

    @pl.loop(0, steps)
    def _(step):
        for copy in fetches(step):
            copy.wait()
        w = weights[step]
        acc[...] += jnp.dot(tokens[step], w[:, : 2 * HEAD], preferred_element_type=F32)
        qacc[...] += jnp.dot(
            tokens[step, : 2 * count], w[:, 2 * HEAD :], preferred_element_type=F32
        )

    kg, qg = kg_ref[...], qg_ref[...]
    k = unit(acc[pl.ds(2 * count, far), :HEAD], kg).astype(BF16)
    v = acc[pl.ds(2 * count, far), HEAD:].astype(BF16)
    for out_ref in (forward_ref, backward_ref, far_ref):
        out_ref[pl.ds(0, far), :HEAD] = k
        out_ref[pl.ds(0, far), HEAD:] = v
    me = me_ref[0]
    lines = pl.ds(far, count)
    for slab, out_ref in enumerate((backward_ref, forward_ref)):
        mine = pl.ds(pl.multiple_of((slab ^ me) * count, count), count)
        out_ref[lines, :HEAD] = unit(acc[mine, :HEAD], kg).astype(BF16)
        out_ref[lines, HEAD:] = acc[mine, HEAD:].astype(BF16)
        q_ref[slab] = unit(qacc[mine], qg).astype(BF16)


def project(me, slabs, styles, w, query_gain, key_gain):
    parts, count, width = slabs[0].shape
    groups, _, rows, _ = styles[0].shape
    pieces = 2
    steps = parts // pieces
    far = 2 * groups * rows
    total = 2 * count + far
    shapes = [(far + count, 2 * HEAD)] * 2 + [(far, 2 * HEAD), (2, count, HEAD)]
    vmem = pl.BlockSpec(memory_space=pltpu.VMEM)
    hbm = pl.BlockSpec(memory_space=pltpu.HBM)
    return pl.pallas_call(
        project_kernel,
        in_specs=[pl.BlockSpec(memory_space=pltpu.SMEM)] + [hbm] * 5 + [vmem] * 2,
        out_specs=[vmem] * len(shapes),
        out_shape=[jax.ShapeDtypeStruct(shape, BF16) for shape in shapes],
        scratch_shapes=[
            pltpu.VMEM((total, 2 * HEAD), F32),
            pltpu.VMEM((2 * count, HEAD), F32),
            pltpu.VMEM((steps, total, pieces * width), BF16),
            pltpu.VMEM((steps, pieces * width, 3 * HEAD), BF16),
            pltpu.SemaphoreType.DMA((steps, 1 + pieces * (2 + 2 * groups))),
        ],
        compiler_params=pltpu.CompilerParams(vmem_limit_bytes=60 << 20),
        name="project",
    )(me, *slabs, *styles, w, query_gain, key_gain)


NT = (((1,), (1,)), ((), ()))


def attend_kernel(
    turn,
    me_ref,
    flag_ref,
    q_ref,
    forward_ref,
    backward_ref,
    before_ref,
    after_ref,
    far_ref,
    o_ref,
    near,
):
    slab = me_ref[0] ^ turn
    count = q_ref.shape[1]
    style = forward_ref.shape[0] - count
    lines = pl.ds(style, count)
    near[pl.ds(0, count)] = backward_ref[lines]
    near[pl.ds(count, count)] = forward_ref[lines]

    @pl.when(slab == 0)
    def _():
        near[pl.ds(2 * count, count)] = before_ref[lines]

    @pl.when(slab == 1)
    def _():
        near[pl.ds(2 * count, count)] = after_ref[lines]

    scale = math.log2(math.e) / math.sqrt(HEAD)
    q = q_ref[slab]
    lines = pl.ds(0, style)
    refs = [near, *(r.at[lines] for r in (forward_ref, before_ref, after_ref)), far_ref]
    scores = []
    for n, ref in enumerate(refs):
        part = lax.dot_general(q, ref[:, :HEAD], NT, preferred_element_type=F32)
        scores.append(jnp.where(flag_ref[0, 0] > 0, part, -1e30) if n else part)
    peak = functools.reduce(jnp.maximum, [jnp.max(s, axis=-1, keepdims=True) for s in scores])
    expo = [jnp.exp2((s - peak) * scale) for s in scores]
    share = 1.0 / sum(jnp.sum(e, axis=-1, keepdims=True) for e in expo)
    o_ref[...] = sum(
        jnp.dot((e * share).astype(BF16), ref[:, HEAD:], preferred_element_type=F32)
        for e, ref in zip(expo, refs)
    ).astype(BF16)


def attend(turn, me, flag, query, *keys):
    count = query.shape[1]
    scalar = pl.BlockSpec(memory_space=pltpu.SMEM)
    vmem = pl.BlockSpec(memory_space=pltpu.VMEM)
    return pl.pallas_call(
        functools.partial(attend_kernel, turn),
        in_specs=[scalar] * 2 + [vmem] * (1 + len(keys)),
        out_specs=vmem,
        out_shape=jax.ShapeDtypeStruct((count, HEAD), BF16),
        scratch_shapes=[pltpu.VMEM((3 * count, 2 * HEAD), BF16)],
        compiler_params=pltpu.CompilerParams(vmem_limit_bytes=24 << 20),
        cost_estimate=pl.CostEstimate(
            flops=11 * 256 * 256 * 4 * HEAD, bytes_accessed=2 << 20, transcendentals=11 << 16
        ),
    )(me, flag, query, *keys)


def mix_kernel(ax_ref, ay_ref, wx_ref, wy_ref, o_ref):
    parts, _, width = o_ref.shape
    a = jnp.concatenate([ax_ref[...], ay_ref[...]], axis=1)
    for i in range(parts):
        lines = pl.ds(i * width, width)
        w = jnp.concatenate([wx_ref[lines], wy_ref[lines]], axis=1)
        o_ref[i] = lax.dot_general(a, w, NT, preferred_element_type=F32).astype(BF16)


def mix(attended, panels, parts):
    count = attended[0].shape[0]
    width = panels[0].shape[0] // parts
    return pl.pallas_call(
        mix_kernel,
        out_shape=jax.ShapeDtypeStruct((parts, count, width), BF16),
        compiler_params=pltpu.CompilerParams(vmem_limit_bytes=12 << 20),
        name="mix",
    )(*attended, *panels)


def local(image_tokens, style_tokens, qkv_weight, out_weight, query_gain, key_gain, attend_flags):
    parts = lax.axis_size(TP)
    cores = lax.axis_size("core")
    halves = lax.axis_size("x_hi")
    rows = lax.axis_size(Z)
    depth = qkv_weight.shape[1]

    def swap(block):
        return lax.ppermute(block, "core", [(0, 1), (1, 0)])

    me = lax.axis_index("core").reshape(1)
    mine = pack(qkv_weight, out_weight.T, halves)
    plane = lax.all_to_all(mine, ("x_hi", "core"), 0, 0, tiled=True)
    plane = plane.reshape(halves, cores * depth, 4 * HEAD)
    panel = lax.all_gather(plane, Z, axis=1, tiled=True).reshape(-1, 4 * HEAD)

    image_tokens, style_tokens, attend_flags, _ = lax.optimization_barrier(
        (image_tokens, style_tokens, attend_flags, plane)
    )

    def shift(block, axes, count, by):
        return lax.ppermute(block, axes, [(i, (i + by) % count) for i in range(count)])

    step = rows // 4
    style = [style_tokens]
    style += [shift(style_tokens, Z, rows, i * step) for i in (1, 2, 3)]
    style = jnp.concatenate(style, axis=0)
    own = spread(image_tokens, TP)
    slabs = (own, swap(own))
    style = spread(style, ("x_hi",) + TP)
    style = style.reshape((halves, parts) + style.shape[1:])
    styles = (style, swap(style))
    flags = (attend_flags, swap(attend_flags))
    slabs, styles, flags = lax.optimization_barrier((slabs, styles, flags))

    forward, backward, far, query = project(
        me, slabs, styles, panel, query_gain.reshape(1, HEAD), key_gain.reshape(1, HEAD)
    )
    chips = halves * rows
    before = shift(forward, ("x_hi",) + Z, chips, 1)
    after = shift(backward, ("x_hi",) + Z, chips, -1)
    pairs = [
        (i * cores + c, (i + 2 - 4 * c) % rows * cores + c) for i in range(rows) for c in (0, 1)
    ]
    far = lax.ppermute(far, Z + ("core",), pairs)
    panel, query = lax.optimization_barrier((panel, query))
    out_own = panel[:, 3 * HEAD :]
    out_other = swap(out_own)

    keys = (forward, backward, before, after, far)
    theirs = swap(attend(1, me, flags[1], query, *keys))
    mine = attend(0, me, flags[0], query, *keys)
    shares = mix((mine, theirs), (out_own, out_other), parts)
    shares = lax.all_to_all(shares, TP, 0, 0, tiled=True)
    return jnp.sum(shares.astype(F32), axis=0).astype(BF16)


def solution(mesh):
    fine = Mesh(mesh.devices.reshape(2, 4, 4, 2, 4, 2), AXES)
    in_specs = (
        P(LON, TP),
        P(LON, TP),
        P(None, LON, TP),
        P(TP, LON),
        P(),
        P(),
        P(LON, None),
    )
    return jax.shard_map(
        local, mesh=fine, in_specs=in_specs, out_specs=P(LON, TP), check_vma=False
    )
```
